32 devices in a mesh: dom: 16 (over z, y, x), wav: 2 (over core).
Axes of the slice: x: 2, y: 2, z: 4, core: 2. Of those that a mesh axis runs over, the one named last changes fastest.
Arguments:
- node_features: bfloat16 [16384, 128], P('dom'), may hold values from -6 to 6
- positions: float32 [3, 16384], P(None, 'dom'), may hold values from 0 to 1, as said below
- neighbours: int32 [128, 8], P('dom'), may hold values from 0 to 15, as said below
- wavevectors: int32 [3, 8192], P(None, 'wav'), may hold values from -8 to 8
- message_weight: bfloat16 [1, 128, 128], replicated, may hold values from -0.5 to 0.5
- spectral_mix: float32 [1, 128, 128], replicated, may hold values from -0.5 to 0.5
- spectral_filter: float32 [1, 8192, 128], P(None, 'wav'), may hold values from 0.2 to 2
Outputs:
- features_out: bfloat16 [16384, 128], P('dom')
The draws below stay inside these ranges and needn't reach their ends.
Inputs may be any that keep to these rules, and one draw needn't show every extreme that they name: `positions`: atom a lies in the unit box with its first coordinate in [d / (number of domains), (d + 1) / (number of domains)) for d = a // 1024; the box is periodic. `neighbours`: each row names 8 different blocks, within 4 places of the row's own block (b mod 8) + 4 in the extended list.
All inputs are finite; a program needn't handle non-finite values.
Results may differ from the reference program's by a relative error of at most 0.0045.
Values may be sent and summed in bfloat16 or wider, within the bound.
No kernel may reach another device: no remote copies, remote signals or barrier semaphores. Data moves between devices by JAX's collectives and lax.ppermute only.
A program may use at most 64 MiB of HBM per device.

```python
import math
import jax
import jax.numpy as jnp
from jax import lax

ATOM_DEV = 1024
CH = 128
KV = 8192
BLOCK = 128
NBR = 8
HALO_BLK = 4
LAYERS = 1
ATOMS = 16384
BLK_DEV = 8
BLOCKS = 128


def draw_positions(key, part):
    unit = jax.random.uniform(key, (3, ATOMS), jnp.float32)
    domain = (jnp.arange(ATOMS, dtype=jnp.int32) // ATOM_DEV).astype(jnp.float32)
    first = (domain + unit[0]) / float(ATOMS // ATOM_DEV)
    return jnp.stack([first, unit[1], unit[2]]).astype(jnp.float32)


def draw_neighbours(key, part):
    keys = jax.random.split(key, BLOCKS)
    offsets = jax.vmap(lambda single: jax.random.permutation(single, 2 * HALO_BLK + 1))(keys)[:, :NBR]
    local = (jnp.arange(BLOCKS, dtype=jnp.int32) % BLK_DEV)[:, None]
    return (local + offsets.astype(jnp.int32)).astype(jnp.int32)


def touch_ends(entries, stream_key, low, top_value):
    longest = entries.shape.index(max(entries.shape))
    spots = []
    for shift in (0, 1):
        where = [jax.random.randint(jax.random.fold_in(stream_key, axis), (), 0, length) for axis, length in enumerate(entries.shape)]
        where[longest] = (where[longest] + shift) % entries.shape[longest]
        spots.append(tuple(where))
    return entries.at[spots[0]].set(low).at[spots[1]].set(top_value)


def steps_of(stream_key, shape, cuts, low, top_value):
    loudness, own = 1.0, jax.random.fold_in(stream_key, 6)
    for position, parts in cuts:
        heights = jnp.exp(jax.random.uniform(jax.random.fold_in(own, position), (parts,), jnp.float32, low / len(cuts), top_value / len(cuts)))
        loudness = loudness * jnp.repeat(heights, shape[position] // parts).reshape([-1 if axis == position else 1 for axis in range(len(shape))])
    return loudness


def noise(key, extent, deviation, limit, cuts=(), kind=jnp.bfloat16):
    array = deviation * jax.random.normal(key, extent, jnp.float32)
    if cuts:
        array = array * steps_of(key, extent, cuts, -0.22, 0.18)
    return jnp.clip(array, -limit, limit).astype(kind)


def setup_inputs(seed: int = 0) -> dict:
    seeds = jax.random.split(jax.random.key(seed), 8)
    return {
        "node_features": noise(seeds[0], (ATOMS, CH), 1.0, 6.0, ((0, 16),)),
        "positions": draw_positions(jax.random.fold_in(seeds[7], 71), 0),
        "neighbours": draw_neighbours(jax.random.fold_in(seeds[7], 71), 0),
        "wavevectors": touch_ends(jax.random.randint(seeds[3], (3, KV), -8, 9), jax.random.fold_in(seeds[3], 1), -8, 8).astype(jnp.int32),
        "message_weight": noise(seeds[4], (LAYERS, CH, CH), CH ** -0.5, 0.5),
        "spectral_mix": noise(seeds[5], (LAYERS, CH, CH), CH ** -0.5, 0.5, (), jnp.float32),
        "spectral_filter": jnp.clip(jnp.exp(math.log(2.0) - 2.3025851 * jax.random.uniform(seeds[6], (LAYERS, KV, CH), jnp.float32) ** steps_of(seeds[6], (LAYERS, KV, CH), ((1, 2),), -0.2, 0.2)), 0.2, 2.0),
    }


TWO_PI = 2.0 * math.pi
KERNEL_DECAY = 12.0
PAIR_SCALE = 1.0 / 16.0

def make_phases(wave, coords):
    angle = TWO_PI * (wave[0][:, None] * coords[0][None, :] + wave[1][:, None] * coords[1][None, :] + wave[2][:, None] * coords[2][None, :])
    return (jnp.cos(angle).astype(jnp.bfloat16), jnp.sin(angle).astype(jnp.bfloat16))

def pair_block(recv_pos, send_pos, senders):
    delta = recv_pos[:, :, :, None] - send_pos[:, :, None, :]
    delta = delta - jnp.floor(delta + 0.5)
    distance = lax.optimization_barrier(jnp.sum(delta * delta, axis=0))
    kernel = jnp.exp(-KERNEL_DECAY * distance).astype(jnp.bfloat16)
    summed = jnp.einsum('bij,bjc->bic', kernel.astype(jnp.float32), senders.astype(jnp.float32))
    return summed * PAIR_SCALE

def reference(node_features, positions, neighbours, wavevectors, message_weight, spectral_mix, spectral_filter):
    domain_of = jnp.arange(BLOCKS, dtype=jnp.int32) // BLK_DEV
    sender = ((domain_of[:, None] * BLK_DEV - HALO_BLK + neighbours) % BLOCKS).astype(jnp.int32)
    pos_blocks = positions.reshape(3, BLOCKS, BLOCK)
    send_pos = pos_blocks[:, sender].reshape(3, BLOCKS // BLK_DEV, BLK_DEV, NBR * BLOCK)
    send_pos = jnp.transpose(send_pos, (1, 0, 2, 3))
    recv_pos = jnp.transpose(pos_blocks.reshape(3, BLOCKS // BLK_DEV, BLK_DEV, BLOCK), (1, 0, 2, 3))
    kb_size = min(KV, 256)
    count = KV // kb_size
    wave_blocks = jnp.transpose(wavevectors.astype(jnp.float32).reshape(3, count, kb_size), (1, 0, 2))
    inv_atoms = 1.0 / math.sqrt(ATOMS)
    inv_waves = 1.0 / math.sqrt(KV)
    features = node_features
    for layer in range(LAYERS):
        values = jnp.dot(features, message_weight[layer], preferred_element_type=jnp.float32).astype(jnp.bfloat16)
        senders = values.reshape(BLOCKS, BLOCK, CH)[sender].reshape(BLOCKS // BLK_DEV, BLK_DEV, NBR * BLOCK, CH)
        short = lax.map(lambda item: pair_block(item[0], item[1], item[2]), (recv_pos, send_pos, senders))
        short = short.reshape(ATOMS, CH)
        mixing = spectral_mix[layer]
        filter_blocks = spectral_filter[layer].reshape(count, kb_size, CH)

        def wave_step(total, item):
            wave, weights = item
            cosines, sines = make_phases(wave, positions)
            spec_cos = jnp.dot(cosines, features, preferred_element_type=jnp.float32) * inv_atoms
            spec_sin = jnp.dot(sines, features, preferred_element_type=jnp.float32) * inv_atoms
            filt_cos = (jnp.dot(spec_cos, mixing, precision=lax.Precision.HIGHEST) * weights).astype(jnp.bfloat16)
            filt_sin = (jnp.dot(spec_sin, mixing, precision=lax.Precision.HIGHEST) * weights).astype(jnp.bfloat16)
            total = total + jnp.dot(cosines.T, filt_cos, preferred_element_type=jnp.float32)
            total = total + jnp.dot(sines.T, filt_sin, preferred_element_type=jnp.float32)
            return (total, None)
        long_sum, unused = lax.scan(wave_step, jnp.zeros((ATOMS, CH), jnp.float32), (wave_blocks, filter_blocks))
        total = short + long_sum * inv_waves
        features = (features.astype(jnp.float32) + jax.nn.silu(total)).astype(jnp.bfloat16)
    return features
```

```python
import math

import jax
import jax.numpy as jnp
import numpy as np
from jax import lax
from jax.experimental import pallas as pl
from jax.experimental.pallas import tpu as pltpu
from jax.sharding import PartitionSpec as P

KV = 8192
BLOCK = 128
NBR = 8
HALO_BLK = 4
TOP = 8
SPAN = 2 * TOP + 1
ROWS8 = 8

TWO_PI = 2.0 * math.pi
KERNEL_DECAY = 12.0
PAIR_SCALE = 1.0 / 16.0

Q_LOW = TOP * SPAN + TOP
Q_ROWS = -(-(2 * Q_LOW + 1) // ROWS8) * ROWS8
Q_TILES = Q_ROWS // ROWS8
FIRST_TILE = Q_LOW // ROWS8
ZERO_TILES = Q_TILES - FIRST_TILE
ALL_TILES = ZERO_TILES + TOP * Q_TILES
assert Q_LOW % ROWS8 == 0

F32 = jnp.float32
BF16 = jnp.bfloat16


def tile_place(tile):
    tile = jnp.minimum(tile, ALL_TILES - 1)
    later = tile - ZERO_TILES
    upper = 1 + jnp.maximum(later, 0) // Q_TILES
    first = later < 0
    n2 = jnp.where(first, 0, upper)
    return n2, jnp.where(first, FIRST_TILE + tile, later - (upper - 1) * Q_TILES)


def selectors():
    q = np.arange(Q_ROWS) - Q_LOW
    n0 = np.floor_divide(q + TOP, SPAN)
    n1 = q - SPAN * n0
    out = []
    for n in (n0, n1):
        hot = (np.abs(n)[:, None] == np.arange(2 * ROWS8)[None, :]).astype(np.float32)
        out += [hot, hot * np.sign(n)[:, None].astype(np.float32)]
    return np.stack(out)


def times(a, b):
    return a[0] * b[0] - a[1] * b[1], a[0] * b[1] + a[1] * b[0]


def fill_tables(pos_ref, sel_ref, xyc_ref, xys_ref, zc_ref, zs_ref, rows_ref):
    angle = TWO_PI * pos_ref[...]
    power = [(jnp.ones_like(angle), jnp.zeros_like(angle)), (jnp.cos(angle), jnp.sin(angle))]
    for n in range(2, TOP + 2):
        power.append(times(power[n // 2], power[n - n // 2]))
    rows_ref[...] = jnp.zeros_like(rows_ref)
    for n, (c, s) in enumerate(power):
        for axis in range(2):
            rows_ref[2 * axis, n : n + 1, :] = c[axis : axis + 1, :]
            rows_ref[2 * axis + 1, n : n + 1, :] = s[axis : axis + 1, :]
        if n <= TOP:
            wide = (ROWS8, angle.shape[1])
            zc_ref[n * ROWS8 : (n + 1) * ROWS8, :] = jnp.broadcast_to(c[2:3, :], wide)
            zs_ref[n * ROWS8 : (n + 1) * ROWS8, :] = jnp.broadcast_to(s[2:3, :], wide)

    def pick(i):
        return jnp.dot(
            sel_ref[i], rows_ref[i], precision=lax.Precision.HIGHEST, preferred_element_type=F32
        )

    xyc_ref[...], xys_ref[...] = times((pick(0), pick(1)), (pick(2), pick(3)))


def fill_phases(first_tile, count, xyc_ref, xys_ref, zc_ref, zs_ref, out_ref):
    def one(i, carry):
        n2, qt = tile_place(first_tile(i))
        q_at = pl.ds(pl.multiple_of(qt * ROWS8, ROWS8), ROWS8)
        z_at = pl.ds(pl.multiple_of(n2 * ROWS8, ROWS8), ROWS8)
        c, s = times((xyc_ref[q_at, :], xys_ref[q_at, :]), (zc_ref[z_at, :], zs_ref[z_at, :]))
        at = pl.ds(pl.multiple_of(i * 2 * ROWS8, 2 * ROWS8), 2 * ROWS8)
        out_ref[at, :] = jnp.concatenate([c, s], axis=0).astype(BF16)
        return carry

    lax.fori_loop(0, count, one, 0, unroll=math.gcd(count, 10))


def spectrum_kernel(which, scale, slices, tiles, doms, build, places, *refs):
    if build:
        pos_ref, sel_ref, h_ref, p_ref, s_ref, xyc, xys, zc, zs, rows = refs

        @pl.when(pl.program_id(0) == 0)
        def _():
            fill_tables(pos_ref, sel_ref, xyc, xys, zc, zs, rows)
    else:
        xyc, xys, zc, zs, h_ref, p_ref, s_ref = refs
    step = pl.program_id(0)

    def tile(i):
        position = which + step * slices + i // tiles
        return (places[1] * doms + (position ^ places[0])) * tiles + i % tiles

    fill_phases(tile, slices * tiles, xyc, xys, zc, zs, p_ref)
    summed = jnp.dot(p_ref[...], h_ref[...], preferred_element_type=F32)
    s_ref[...] = (summed * scale).astype(s_ref.dtype)


def spectrum_half(places, upper, tables, features, scale, doms, tiles, dtype):
    atoms, channels = features.shape
    half = doms // 2
    steps = min(4, half)
    slices = half // steps
    rows = slices * tiles * 2 * ROWS8
    whole = lambda *shape: pl.BlockSpec(shape, lambda i, p: (0,) * len(shape))
    table = [(Q_ROWS, atoms), (Q_ROWS, atoms), ((TOP + 1) * ROWS8, atoms), ((TOP + 1) * ROWS8, atoms)]
    out_specs = [
        pl.BlockSpec((rows, atoms), lambda i, p: (i, 0)),
        pl.BlockSpec((rows, channels), lambda i, p: (i, 0)),
    ]
    out_shape = [
        jax.ShapeDtypeStruct((rows * steps, atoms), BF16),
        jax.ShapeDtypeStruct((rows * steps, channels), dtype),
    ]
    scratch = []
    if upper:
        out_specs += [whole(*shape) for shape in table]
        out_shape += [jax.ShapeDtypeStruct(shape, F32) for shape in table]
        scratch = [pltpu.VMEM((4, 2 * ROWS8, atoms), F32)]
    body = lambda *refs: spectrum_kernel(
        half if upper else 0, scale, slices, tiles, doms, upper, *refs
    )
    return pl.pallas_call(
        body,
        grid_spec=pltpu.PrefetchScalarGridSpec(
            num_scalar_prefetch=1,
            grid=(steps,),
            in_specs=[whole(*t.shape) for t in tables] + [whole(atoms, channels)],
            out_specs=out_specs,
            scratch_shapes=scratch,
        ),
        out_shape=out_shape,
        name="spectrum_upper" if upper else "spectrum_lower",
    )(places, *tables, features)


def weights_kernel(tiles, bases, wave_ref, filter_ref, out_ref, hot_ref):
    n0, n1, n2 = wave_ref[0:1, :], wave_ref[1:2, :], wave_ref[2:3, :]
    q = SPAN * n0 + n1
    flip = jnp.logical_or(n2 < 0, jnp.logical_and(n2 == 0, q < 0))
    key = jnp.where(flip, -n2, n2) * Q_ROWS + jnp.where(flip, -q, q) + Q_LOW
    wide = jnp.broadcast_to(key, (ROWS8, key.shape[1]))
    row = lax.broadcasted_iota(jnp.int32, wide.shape, 0)
    shifted = wide - row
    for t in range(0, tiles, 2):
        both = [
            jnp.where(shifted == bases[u], 1.0, 0.0).astype(F32) for u in (t, t + 1)
        ]
        hot_ref[t * ROWS8 : (t + 2) * ROWS8, :] = jnp.concatenate(both, axis=0).astype(BF16)
    w = filter_ref[...]
    high = w.astype(BF16)
    low = (w - high.astype(F32)).astype(BF16)
    hot = hot_ref[...]
    part = jnp.dot(hot, high, preferred_element_type=F32) + jnp.dot(
        hot, low, preferred_element_type=F32
    )

    @pl.when(pl.program_id(0) == 0)
    def _():
        out_ref[...] = part

    @pl.when(pl.program_id(0) != 0)
    def _():
        out_ref[...] += part


def lattice_weights(bases, wavevectors, weights):
    tiles = bases.shape[0]
    waves, channels = weights.shape
    steps = 4 if waves % (4 * BLOCK) == 0 else 1
    chunk = waves // steps
    return pl.pallas_call(
        lambda *refs: weights_kernel(tiles, *refs),
        grid_spec=pltpu.PrefetchScalarGridSpec(
            num_scalar_prefetch=1,
            grid=(steps,),
            in_specs=[
                pl.BlockSpec((3, chunk), lambda i, b: (0, i)),
                pl.BlockSpec((chunk, channels), lambda i, b: (i, 0)),
            ],
            out_specs=pl.BlockSpec((tiles * ROWS8, channels), lambda i, b: (0, 0)),
            scratch_shapes=[pltpu.VMEM((tiles * ROWS8, chunk), BF16)],
        ),
        out_shape=jax.ShapeDtypeStruct((tiles * ROWS8, channels), F32),
        name="lattice_weights",
    )(bases, wavevectors, weights)


def filter_kernel(mine_ref, other_ref, mix_ref, *refs):
    *weight_refs, out_ref = refs
    rows = mine_ref.shape[0]
    half = rows // 2
    other = other_ref[...].astype(F32)
    total = mine_ref[...] + jnp.concatenate([other[half:], other[:half]], axis=0)
    mixed = jnp.dot(
        total, mix_ref[...], precision=lax.Precision.HIGHEST, preferred_element_type=F32
    )
    weights = weight_refs[0][...]
    for ref in weight_refs[1:]:
        weights = weights + ref[...]
    groups = rows // (2 * ROWS8)
    mixed = mixed.reshape(groups, 2, ROWS8, -1) * weights.reshape(groups, 1, ROWS8, -1)
    out_ref[...] = mixed.reshape(rows, -1).astype(BF16)


def filtered(mine, other, mixing, weights):
    return pl.pallas_call(
        filter_kernel,
        out_shape=jax.ShapeDtypeStruct(mine.shape, BF16),
        name="filter_rows",
    )(mine, other, mixing, *weights)


def pack_kernel(places, pos_ref, h_ref, out_ref):
    rows = h_ref.shape[0]
    out_ref[0:rows, :] = h_ref[...]
    pos = pos_ref[...]
    high = pos.astype(BF16).astype(F32)
    mid = (pos - high).astype(BF16).astype(F32)
    low = pos - high - mid
    blocks = rows // BLOCK
    parts = []
    for part in (high, mid, low):
        for axis in range(3):
            for b in range(blocks):
                parts.append(part[axis : axis + 1, b * BLOCK : (b + 1) * BLOCK])
    parts += [jnp.zeros_like(parts[0])] * (out_ref.shape[0] - rows - len(parts))
    out_ref[rows:, :] = jnp.concatenate(parts, axis=0).astype(BF16)


def packed_half(places, positions, features, rows):
    extra = -(-9 * (rows // BLOCK) // (2 * ROWS8)) * 2 * ROWS8
    return pl.pallas_call(
        pack_kernel,
        grid_spec=pltpu.PrefetchScalarGridSpec(
            num_scalar_prefetch=1,
            grid=(1,),
            in_specs=[
                pl.BlockSpec((3, rows), lambda i, p: (0, p[1])),
                pl.BlockSpec((rows, features.shape[1]), lambda i, p: (p[1], 0)),
            ],
            out_specs=pl.BlockSpec((rows + extra, features.shape[1]), lambda i, p: (0, 0)),
        ),
        out_shape=jax.ShapeDtypeStruct((rows + extra, features.shape[1]), BF16),
        name="pack_half",
    )(places, positions, features)


def short_kernel(halo_blocks, lists, pos_ref, h_ref, halo_ref, weight_ref, out_ref, val_ref, at_ref):
    own = h_ref.shape[0] // BLOCK
    share = out_ref.shape[0] // BLOCK
    rows = halo_blocks * BLOCK
    weight = weight_ref[...]
    val_ref[0 : own * BLOCK, :] = jnp.dot(
        h_ref[...], weight, preferred_element_type=F32
    ).astype(BF16)
    val_ref[own * BLOCK :, :] = jnp.dot(
        halo_ref[0:rows, :], weight, preferred_element_type=F32
    ).astype(BF16)
    pieces = halo_ref[rows:, :].astype(F32)
    n = 3 * halo_blocks
    there = pieces[0:n] + pieces[n : 2 * n] + pieces[2 * n : 3 * n]
    for axis in range(3):
        for b in range(own):
            at_ref[b, axis : axis + 1, :] = pos_ref[axis : axis + 1, b * BLOCK : (b + 1) * BLOCK]
        for b in range(halo_blocks):
            at_ref[own + b, axis : axis + 1, :] = there[
                axis * halo_blocks + b : axis * halo_blocks + b + 1, :
            ]
    first = lists[share * NBR]

    def block(b, carry):
        columns = jnp.transpose(at_ref[first + b])
        total = jnp.zeros((BLOCK, out_ref.shape[1]), F32)
        for m in range(NBR):
            sender = lists[b * NBR + m]
            sent = at_ref[sender]
            distance = None
            for axis in range(3):
                delta = columns[:, axis : axis + 1] - sent[axis : axis + 1, :]
                delta = delta - jnp.floor(delta + 0.5)
                square = delta * delta
                distance = square if distance is None else distance + square
            kernel = jnp.exp(-KERNEL_DECAY * distance).astype(BF16)
            at = pl.ds(pl.multiple_of(sender * BLOCK, BLOCK), BLOCK)
            total = total + jnp.dot(kernel, val_ref[at, :], preferred_element_type=F32)
        out_ref[pl.ds(pl.multiple_of(b * BLOCK, BLOCK), BLOCK), :] = total * PAIR_SCALE
        return carry

    lax.fori_loop(0, share, block, 0)


def short_messages(lists, positions, features, halo, weight, halo_blocks, share):
    own = features.shape[0] // BLOCK
    channels = features.shape[1]
    whole = lambda a: pl.BlockSpec(a.shape, lambda i, p: (0,) * a.ndim)
    return pl.pallas_call(
        lambda *refs: short_kernel(halo_blocks, *refs),
        grid_spec=pltpu.PrefetchScalarGridSpec(
            num_scalar_prefetch=1,
            grid=(1,),
            in_specs=[whole(a) for a in (positions, features, halo, weight)],
            out_specs=pl.BlockSpec((share * BLOCK, channels), lambda i, p: (0, 0)),
            scratch_shapes=[
                pltpu.VMEM(((own + halo_blocks) * BLOCK, channels), BF16),
                pltpu.VMEM((own + halo_blocks, ROWS8, BLOCK), F32),
            ],
        ),
        out_shape=jax.ShapeDtypeStruct((share * BLOCK, channels), F32),
        name="short_range",
    )(lists, positions, features, halo, weight)


def back_project(phases, filt):
    dims = (((0,), (0,)), ((), ()))
    return lax.dot_general(phases, filt, dims, preferred_element_type=F32)


def swap_orders(bits):
    plain = list(range(bits))
    other = plain[2:3] + plain[:2] + plain[3:] if bits > 3 else plain[1:2] + plain[:1] + plain[2:]
    return plain, other


def neighbour_values(array, width):
    size, length = lax.axis_size("dom"), array.shape[0]
    up = [(i, (i + 1) % size) for i in range(size)]
    down = [(j, i) for i, j in up]
    before = lax.ppermute(array[length - width :], "dom", up)
    after = lax.ppermute(array[:width], "dom", down)
    return before, after


def local(
    node_features, positions, neighbours, wavevectors, message_weight, spectral_mix, spectral_filter
):
    features = node_features
    atoms, channels = features.shape
    doms, wavs = lax.axis_size("dom"), lax.axis_size("wav")
    dom, wav = lax.axis_index("dom"), lax.axis_index("wav")
    bits = doms.bit_length() - 1
    assert doms == 1 << bits and bits > 2 and wavs & (wavs - 1) == 0
    blocks = atoms // BLOCK
    share = blocks // wavs
    inv_atoms = 1.0 / math.sqrt(atoms * doms)
    inv_waves = 1.0 / math.sqrt(KV)
    tiles = -(-ALL_TILES // (doms * wavs))
    orders = swap_orders(bits)

    def code_of(w):
        codes = []
        for order in orders:
            code = 0
            for step, bit in enumerate(order):
                code = code + (((dom >> bit) & 1) << (bits - 1 - step))
            codes.append(code)
        return jnp.where(w % 2 == 0, codes[0], codes[1])

    def swap(x, step):
        pairs = []
        for d in range(doms):
            for w in range(wavs):
                pairs.append((d * wavs + w, (d ^ (1 << orders[w % 2][step])) * wavs + w))
        return lax.ppermute(x, ("dom", "wav"), pairs)

    def swap_wav(x, mask):
        return lax.ppermute(x, "wav", [(w, w ^ mask) for w in range(wavs)])

    places = jnp.stack([code_of(wav), wav]).astype(jnp.int32)

    if wavs == 2 and share == HALO_BLK:
        packed = packed_half(places, positions, features, share * BLOCK)
        count = doms * wavs
        chain = [(g, (g + 1 if g % 2 else g - 1) % count) for g in range(count)]
        halo = lax.ppermute(packed, ("dom", "wav"), chain)
        halo_blocks = HALO_BLK
    else:
        rim = HALO_BLK * BLOCK
        zero = jnp.zeros((1,), jnp.int32)
        first, last = (
            packed_half(
                jnp.concatenate([zero, zero]),
                positions[:, at : at + rim],
                features[at : at + rim],
                rim,
            )
            for at in (0, atoms - rim)
        )
        size = doms
        up = [(i, (i + 1) % size) for i in range(size)]
        before = lax.ppermute(last, "dom", up)
        after = lax.ppermute(first, "dom", [(j, i) for i, j in up])
        n = 3 * HALO_BLK
        pieces = []
        for k in range(9):
            for side in (before, after):
                pieces.append(side[rim + k * HALO_BLK : rim + (k + 1) * HALO_BLK])
        extra = -(-9 * 2 * HALO_BLK // (2 * ROWS8)) * 2 * ROWS8 - 9 * 2 * HALO_BLK
        halo = jnp.concatenate(
            [before[:rim], after[:rim], *pieces, jnp.zeros((extra, channels), BF16)], axis=0
        )
        halo_blocks = 2 * HALO_BLK
    first_block = wav * share
    ext = lax.dynamic_slice_in_dim(neighbours, first_block, share, 0).reshape(-1)
    inside = jnp.logical_and(ext >= HALO_BLK, ext < HALO_BLK + blocks)
    if halo_blocks == HALO_BLK:
        outside = blocks + ext % (HALO_BLK + blocks)
    else:
        outside = blocks + jnp.where(ext < HALO_BLK, ext, ext - blocks)
    lists = jnp.where(inside, ext - HALO_BLK, outside)
    lists = jnp.concatenate([lists, first_block[None]]).astype(jnp.int32)

    phases_up, leaving, *tables = spectrum_half(
        places, True, [positions, jnp.asarray(selectors())], features, inv_atoms, doms, tiles, BF16
    )
    arrived = swap(leaving, 0)
    phases_low, kept = spectrum_half(places, False, tables, features, inv_atoms, doms, tiles, F32)

    owners = jnp.stack([wav ^ v for v in range(wavs)])
    first_slice = jnp.stack([code_of(w) for w in [wav ^ v for v in range(wavs)]])
    slices = first_slice[:, None] ^ jnp.arange(2)[None, :]
    numbers = (owners[:, None] * doms + slices)[:, :, None] * tiles + jnp.arange(tiles)
    numbers = numbers.reshape(-1)
    n2, qt = tile_place(numbers)
    bases = jnp.where(numbers < ALL_TILES, n2 * Q_ROWS + qt * ROWS8, -Q_ROWS).astype(jnp.int32)
    gathered = lattice_weights(bases, wavevectors, spectral_filter[0])
    mask = wavs // 2
    while mask:
        half = gathered.shape[0] // 2
        other = swap_wav(gathered[half:], mask)
        if mask == 1:
            weights = [gathered[:half], other]
        else:
            gathered = gathered[:half] + other
        mask //= 2

    short = short_messages(
        lists, positions, features, halo, message_weight[0], halo_blocks, share
    )

    for step in range(bits - 1):
        kept = kept + arrived.astype(F32)
        half = kept.shape[0] // 2
        if step + 1 < bits - 1:
            arrived = swap(kept[half:].astype(BF16), step + 1)
            kept = kept[:half]
        else:
            arrived = swap(kept.astype(BF16), step + 1)
    filt = filtered(kept, arrived, spectral_mix[0], weights)
    for step in reversed(range(1, bits - 1)):
        filt = jnp.concatenate([filt, swap(filt, step)], axis=0)
    filt_up = swap(filt, 0)
    total = back_project(phases_low, filt) + back_project(phases_up, filt_up)
    total = total * inv_waves
    row_start = first_block * BLOCK
    mine = lax.dynamic_slice_in_dim(total, row_start, share * BLOCK, 0) + short
    total = lax.dynamic_update_slice_in_dim(total, mine, row_start, 0)
    mask = wavs // 2
    while mask:
        total = total + swap_wav(total, mask)
        mask //= 2
    return (features.astype(F32) + jax.nn.silu(total)).astype(BF16)


def solution(mesh):
    placed = (
        P("dom", None),
        P(None, "dom"),
        P("dom", None),
        P(None, "wav"),
        P(),
        P(),
        P(None, "wav", None),
    )
    return jax.shard_map(
        local, mesh=mesh, in_specs=placed, out_specs=P("dom", None), check_vma=False
    )
```

```python
import math

import jax
import jax.numpy as jnp
from jax import lax
from jax.experimental import pallas as pl
from jax.experimental.pallas import tpu as pltpu
from jax.sharding import PartitionSpec as P


KV = 8192
BLOCK = 128
NBR = 8
HALO_BLK = 4
TOP = 8
SPAN = 2 * TOP + 1

TWO_PI = 2.0 * math.pi
KERNEL_DECAY = 12.0
PAIR_SCALE = 1.0 / 16.0

TILE = 8
CHAINS = 2
Q_TILES = 2 * SPAN + 3
Q_ROWS = Q_TILES * TILE
FIRST_TILE = 2 + 2 * TOP
ZERO_TILES = Q_TILES - FIRST_TILE
ALL_TILES = ZERO_TILES + TOP * Q_TILES
assert TOP == TILE

F32 = jnp.float32
BF16 = jnp.bfloat16
VMEM = pltpu.VMEM


def in_vmem(array):
    return pltpu.with_memory_space_constraint(array, VMEM)


def call(body, out, *args, smem=(), scratch=(), limit=16):
    spec = pl.BlockSpec(memory_space=VMEM)
    specs = [spec] * len(args) + [pl.BlockSpec(memory_space=pltpu.SMEM)] * len(smem)
    single = not isinstance(out, (list, tuple))
    return pl.pallas_call(
        body,
        in_specs=specs,
        out_specs=spec if single else [spec] * len(out),
        out_shape=out,
        scratch_shapes=list(scratch),
        compiler_params=pltpu.CompilerParams(vmem_limit_bytes=limit << 20),
    )(*[in_vmem(a) for a in args], *smem)


DIVIDE = -(-(1 << 16) // Q_TILES)
assert all((v * DIVIDE) >> 16 == v // Q_TILES for v in range(ALL_TILES))


class Layout:
    def __init__(self, atoms):
        self.atoms = atoms
        self.doms, self.wavs = lax.axis_size("dom"), lax.axis_size("wav")
        self.bits = self.doms.bit_length() - 1
        assert self.doms == 1 << self.bits and self.bits > 3
        assert self.wavs & (self.wavs - 1) == 0
        self.tiles = -(-ALL_TILES // (self.doms * self.wavs * CHAINS))
        self.slice_rows = 2 * TILE * self.tiles
        self.rows = self.slice_rows * self.doms

    def order(self, wav, chain):
        turn = (0, 1, 2, 0)[(CHAINS * wav + chain) % 4]
        first = [0, 1, 2]
        return first[turn:] + first[:turn] + list(range(3, self.bits))

    def code(self, wav, chain):
        dom = lax.axis_index("dom")
        codes = []
        for w in (0, 1):
            code = 0
            for step, bit in enumerate(self.order(w, chain)):
                code = code | (((dom >> bit) & 1) << (self.bits - 1 - step))
            codes.append(code)
        return jnp.where((wav & 1) == 0, codes[0], codes[1])

    def first_tile(self, wav, chain, position):
        number = CHAINS * wav + chain
        return (number * self.doms + (position ^ self.code(wav, chain))) * self.tiles


def tile_place(tile):
    tile = jnp.minimum(tile, ALL_TILES - 1)
    later = tile - ZERO_TILES
    first = later < 0
    plane = (jnp.maximum(later, 0) * DIVIDE) >> 16
    n2 = jnp.where(first, 0, 1 + plane)
    return n2, jnp.where(first, FIRST_TILE + tile, later - plane * Q_TILES)


def times(a, b):
    return a[0] * b[0] - a[1] * b[1], a[0] * b[1] + a[1] * b[0]


def fill_tables(pos_ref, xyc_ref, xys_ref, zc_ref, zs_ref):
    angle = TWO_PI * pos_ref[...]
    power = [(jnp.ones_like(angle), jnp.zeros_like(angle)), (jnp.cos(angle), jnp.sin(angle))]
    for n in range(2, TOP + 1):
        power.append(times(power[n // 2], power[n - n // 2]))
    wide = (TILE, angle.shape[1])

    def row(n, axis):
        c, s = power[abs(n)]
        c, s = c[axis : axis + 1, :], s[axis : axis + 1, :]
        return c, (s if n >= 0 else -s)

    def spread(n, axis):
        return tuple(jnp.broadcast_to(v, wide) for v in row(n, axis))

    def stack(numbers, axis):
        rows = [row(n, axis) for n in numbers]
        return tuple(jnp.concatenate([r[i] for r in rows], axis=0) for i in (0, 1))

    for n in range(TOP + 1):
        at = slice(n * TILE, (n + 1) * TILE)
        zc_ref[at, :], zs_ref[at, :] = spread(n, 2)

    def put(tile, a, b):
        at = slice(tile * TILE, (tile + 1) * TILE)
        xyc_ref[at, :], xys_ref[at, :] = times(a, b)

    below, above = stack(range(-TOP, 0), 1), stack(range(TOP), 1)
    edge = spread(TOP, 1)
    for n in range(-TOP, TOP + 1):
        here = spread(n, 0)
        put(1 + 2 * (n + TOP), here, below)
        put(2 + 2 * (n + TOP), here, above)
    put(0, stack(range(-TOP, 0), 0), edge)
    put(Q_TILES - 2, stack(range(TOP), 0), edge)
    put(Q_TILES - 1, spread(TOP, 0), edge)


def fill_phases(lay, chain, low, count, tables, h_ref, p_ref, p_at, put):
    xyc_ref, xys_ref, zc_ref, zs_ref = tables
    wav = lax.axis_index("wav")
    group = max(1, count // 2)
    rows = group * lay.slice_rows
    feats = h_ref[...]

    def chunk(step, carry):
        start = pl.multiple_of(step * rows, rows)
        for part in range(group):
            base = lay.first_tile(wav, chain, low + step * group + part)
            for i in range(lay.tiles):
                n2, qt = tile_place(base + i)
                q_at = pl.ds(pl.multiple_of(qt * TILE, TILE), TILE)
                z_at = pl.ds(pl.multiple_of(n2 * TILE, TILE), TILE)
                c, s = times((xyc_ref[q_at, :], xys_ref[q_at, :]), (zc_ref[z_at, :], zs_ref[z_at, :]))
                at = p_at + start + (part * lay.tiles + i) * 2 * TILE
                at = pl.ds(pl.multiple_of(at, 2 * TILE), 2 * TILE)
                p_ref[at, :] = jnp.concatenate([c, s], axis=0).astype(BF16)
        here = pl.ds(pl.multiple_of(p_at + start, rows), rows)
        put(pl.ds(start, rows), jnp.dot(p_ref[here, :], feats, preferred_element_type=F32))
        return carry

    lax.fori_loop(0, count // group, chunk, 0)


def phase_tables(positions):
    atoms = positions.shape[1]
    table = [(Q_ROWS, atoms)] * 2 + [((TOP + 1) * TILE, atoms)] * 2
    return call(fill_tables, [VMEM(shape, F32) for shape in table], positions)


def spectrum_upper(lay, chain, scale, tables, features):
    half = lay.doms // 2

    def body(xyc, xys, zc, zs, h_ref, p_ref, s_ref):
        def put(at, value):
            s_ref[at, :] = (value * scale).astype(BF16)

        fill_phases(lay, chain, half, half, (xyc, xys, zc, zs), h_ref, p_ref, 0, put)

    out = [VMEM((lay.rows // 2, lay.atoms), BF16), VMEM((lay.rows // 2, features.shape[1]), BF16)]
    return call(body, out, *tables, features)


def spectrum_lower(lay, scale, tables, features):
    def body(xyc, xys, zc, zs, h_ref, p_ref, *s_refs):
        for chain, s_ref in enumerate(s_refs):

            def put(at, value):
                s_ref[at, :] = value * scale

            fill_phases(
                lay, chain, 0, lay.doms // 2, (xyc, xys, zc, zs), h_ref, p_ref,
                chain * (lay.rows // 2), put,
            )

    out = [VMEM((CHAINS * lay.rows // 2, lay.atoms), BF16)]
    out += [VMEM((lay.rows // 2, features.shape[1]), F32)] * CHAINS
    phases, *sums = call(body, out, *tables, features)
    return phases, sums


def lattice_weights(lay, wavevectors, weights):
    waves, channels = weights.shape
    tiles = 2 * lay.tiles * lay.wavs * CHAINS
    chunk = min(waves, 1024)

    def body(wave_ref, filter_ref, *refs):
        *out_refs, hot_ref = refs
        wav = lax.axis_index("wav")
        bases = []
        for v in range(lay.wavs):
            for chain in range(CHAINS):
                for p in range(2):
                    first = lay.first_tile(wav ^ v, chain, p)
                    for i in range(lay.tiles):
                        n2, qt = tile_place(first + i)
                        base = n2 * Q_ROWS + qt * TILE
                        bases.append(jnp.where(first + i < ALL_TILES, base, -Q_ROWS))
        total = None
        for start in range(0, waves, chunk):
            at = slice(start, start + chunk)
            n0, n1, n2 = (wave_ref[a : a + 1, at] for a in range(3))
            negative = jnp.logical_or(n0 < 0, jnp.logical_and(n0 == 0, n1 < 0))
            flip = jnp.logical_or(n2 < 0, jnp.logical_and(n2 == 0, negative))
            n0, n1, n2 = (jnp.where(flip, -n, n) for n in (n0, n1, n2))
            inner = TILE + (n0 + TOP) * 2 * TILE + n1 + TOP
            outer = jnp.where(n0 < 0, n0 + TOP, (Q_TILES - 2) * TILE + n0)
            key = n2 * Q_ROWS + jnp.where(n1 == TOP, outer, inner)
            wide = jnp.broadcast_to(key, (TILE, chunk))
            shifted = wide - lax.broadcasted_iota(jnp.int32, wide.shape, 0)
            for t in range(0, tiles, 2):
                both = [jnp.where(shifted == bases[u], 1.0, 0.0) for u in (t, t + 1)]
                hot_ref[t * TILE : (t + 2) * TILE, :] = jnp.concatenate(both, axis=0).astype(BF16)
            w = filter_ref[at, :]
            high = w.astype(BF16)
            low = (w - high.astype(F32)).astype(BF16)
            part = jnp.dot(
                hot_ref[...], jnp.concatenate([high, low], axis=1), preferred_element_type=F32
            )
            total = part if total is None else total + part
        total = total[:, :channels] + total[:, channels:]
        rows = tiles * TILE // lay.wavs
        for v, ref in enumerate(out_refs):
            ref[...] = total[v * rows : (v + 1) * rows]

    out = [VMEM((tiles * TILE // lay.wavs, channels), F32)] * lay.wavs
    return call(
        body, out, wavevectors, weights,
        scratch=[VMEM((tiles * TILE, chunk), BF16)],
    )


def add_split(mine, other):
    rows, channels = mine.shape

    def body(a_ref, b_ref, keep_ref, send_ref):
        total = a_ref[...] + b_ref[...].astype(F32)
        keep_ref[...] = total[: rows // 2]
        send_ref[...] = total[rows // 2 :].astype(BF16)

    out = [VMEM((rows // 2, channels), F32), VMEM((rows // 2, channels), BF16)]
    return call(body, out, mine, other)


def add_all(mine, others):
    rows, channels = mine[0].shape

    def body(*refs):
        keep_ref, send_ref = refs[-2:]
        for i in range(CHAINS):
            at = slice(i * rows, (i + 1) * rows)
            total = refs[i][...] + refs[CHAINS + i][...].astype(F32)
            keep_ref[at, :] = total
            send_ref[at, :] = total.astype(BF16)

    out = [VMEM((CHAINS * rows, channels), t) for t in (F32, BF16)]
    return call(body, out, *mine, *others)


def add_plain(mine, other):
    def body(a_ref, b_ref, out_ref):
        out_ref[...] = a_ref[...] + b_ref[...].astype(F32)

    return call(body, VMEM(mine.shape, F32), mine, other)


def dot_exact(a, b):
    return jnp.dot(a, b, precision=lax.Precision.HIGHEST, preferred_element_type=F32)


def filtered(mine, other, mixing, weights):
    rows, channels = mine.shape
    part = rows // CHAINS
    groups = rows // (2 * TILE)

    def body(mine_ref, other_ref, mix_ref, *refs):
        weight_refs, out_refs = refs[:-CHAINS], refs[-CHAINS:]
        there = other_ref[...].astype(F32)
        cuts = [there[i * part // 2 : (i + 1) * part // 2] for i in range(2 * CHAINS)]
        there = jnp.concatenate([cuts[i ^ 1] for i in range(2 * CHAINS)], axis=0)
        mixed = dot_exact(mine_ref[...] + there, mix_ref[...])
        factor = weight_refs[0][...]
        for ref in weight_refs[1:]:
            factor = factor + ref[...]
        mixed = mixed.reshape(groups, 2, TILE, channels) * factor.reshape(groups, 1, TILE, channels)
        mixed = mixed.reshape(rows, channels).astype(BF16)
        for i, ref in enumerate(out_refs):
            ref[...] = mixed[i * part : (i + 1) * part]

    out = [VMEM((part, channels), BF16)] * CHAINS
    return call(body, out, mine, other, mixing, *weights)


def join(low, high):
    def body(a_ref, b_ref, out_ref):
        rows = a_ref.shape[0]
        out_ref[:rows, :] = a_ref[...]
        out_ref[rows:, :] = b_ref[...]

    out = VMEM((low.shape[0] + high.shape[0], low.shape[1]), low.dtype)
    return call(body, out, low, high)


def pack_half(positions, features, share):
    rows, channels = share * BLOCK, features.shape[1]
    extra = -(-9 * share // (2 * TILE)) * 2 * TILE

    def body(pos_ref, h_ref, out_ref):
        start = pl.multiple_of(lax.axis_index("wav") * rows, rows)
        out_ref[:rows, :] = h_ref[pl.ds(start, rows), :]
        fill_coordinates(pos_ref[:, pl.ds(start, rows)], out_ref, rows)

    return call(body, VMEM((rows + extra, channels), BF16), positions, features)


def short_range(neighbours, positions, features, halos, weight, share):
    channels = features.shape[1]
    own = features.shape[0] // BLOCK
    near = [HALO_BLK] * len(halos)
    blocks = own + sum(near)
    both = len(halos) == 2

    def body(pos_ref, h_ref, weight_ref, *refs):
        halo_refs, (lists, out_ref, val_ref, at_ref) = refs[: len(halos)], refs[len(halos) :]
        w = weight_ref[...]

        def project(rows):
            return jnp.dot(rows, w, preferred_element_type=F32).astype(BF16)

        val_ref[: own * BLOCK, :] = project(h_ref[...])
        pos = pos_ref[...]
        for b in range(own):
            at_ref[b, 0:3, :] = pos[:, b * BLOCK : (b + 1) * BLOCK]
        at = own
        for ref, count in zip(halo_refs, near):
            rows = count * BLOCK
            val_ref[at * BLOCK : (at + count) * BLOCK, :] = project(ref[:rows, :])
            pieces = ref[rows:, :].astype(F32)
            n = 3 * count
            there = pieces[:n] + pieces[n : 2 * n] + pieces[2 * n : 3 * n]
            for b in range(count):
                for axis in range(3):
                    k = axis * count + b
                    at_ref[at + b, axis : axis + 1, :] = there[k : k + 1]
            at += count
        first = lax.axis_index("wav") * share

        def block(b, carry):
            columns = jnp.transpose(at_ref[first + b])
            total = jnp.zeros((BLOCK, channels), F32)
            for m in range(NBR):
                ext = lists[first + b, m]
                inside = jnp.logical_and(ext >= HALO_BLK, ext < HALO_BLK + own)
                if both:
                    outside = own + jnp.where(ext < HALO_BLK, ext, ext - own)
                else:
                    outside = own + jnp.where(ext < HALO_BLK, ext, ext - HALO_BLK - own)
                sender = jnp.where(inside, ext - HALO_BLK, outside)
                sent = at_ref[sender]
                distance = None
                for axis in range(3):
                    delta = columns[:, axis : axis + 1] - sent[axis : axis + 1, :]
                    delta = delta - jnp.floor(delta + 0.5)
                    square = delta * delta
                    distance = square if distance is None else distance + square
                kernel = jnp.exp(-KERNEL_DECAY * distance).astype(BF16)
                rows = pl.ds(pl.multiple_of(sender * BLOCK, BLOCK), BLOCK)
                total = total + jnp.dot(kernel, val_ref[rows, :], preferred_element_type=F32)
            out_ref[pl.ds(pl.multiple_of(b * BLOCK, BLOCK), BLOCK), :] = total * PAIR_SCALE
            return carry

        lax.fori_loop(0, share, block, 0)

    return call(
        body, VMEM((share * BLOCK, channels), F32), positions, features, weight,
        *halos, smem=[neighbours],
        scratch=[VMEM((blocks * BLOCK, channels), BF16), VMEM((blocks, TILE, BLOCK), F32)],
    )


def transposed_dot(phases, filt):
    dims = (((0,), (0,)), ((), ()))
    return lax.dot_general(phases, filt, dims, preferred_element_type=F32)


def back_lower(phases, filts):
    def body(p_ref, *refs):
        *f_refs, out_ref = refs
        filt = jnp.concatenate([ref[...] for ref in f_refs], axis=0)
        out_ref[...] = transposed_dot(p_ref[...], filt)

    out = VMEM((phases.shape[1], filts[0].shape[1]), F32)
    return call(body, out, phases, *filts)


def back_more(part, phases, filt):
    def body(part_ref, p_ref, f_ref, out_ref):
        out_ref[...] = part_ref[...] + transposed_dot(p_ref[...], f_ref[...])

    return call(body, VMEM(part.shape, F32), part, phases, filt)


def back_last(part, phases, filt, short, scale):
    rows = short.shape[0]

    def body(part_ref, p_ref, f_ref, short_ref, out_ref, send_ref):
        out_ref[...] = (part_ref[...] + transposed_dot(p_ref[...], f_ref[...])) * scale
        here = pl.ds(pl.multiple_of(lax.axis_index("wav") * rows, rows), rows)
        out_ref[here, :] += short_ref[...]
        send_ref[...] = out_ref[...].astype(BF16)

    out = [VMEM(part.shape, t) for t in (F32, BF16)]
    return call(body, out, part, phases, filt, short)


def finish(features, total, other):
    def body(h_ref, a_ref, b_ref, out_ref):
        total = a_ref[...] + b_ref[...].astype(F32)
        out_ref[...] = (h_ref[...].astype(F32) + total * jax.nn.sigmoid(total)).astype(BF16)

    out = jax.ShapeDtypeStruct(features.shape, BF16)
    return call(body, out, features, total, other)


def local(
    node_features, positions, neighbours, wavevectors, message_weight, spectral_mix, spectral_filter
):
    features = node_features
    atoms = features.shape[0]
    lay = Layout(atoms)
    doms, wavs, bits = lay.doms, lay.wavs, lay.bits
    blocks = atoms // BLOCK
    share = blocks // wavs
    inv_atoms = 1.0 / math.sqrt(atoms * doms)
    inv_waves = 1.0 / math.sqrt(KV)

    def swap(x, chain, step):
        pairs = []
        for d in range(doms):
            for w in range(wavs):
                pairs.append((d * wavs + w, (d ^ (1 << lay.order(w, chain)[step])) * wavs + w))
        return lax.ppermute(x, ("dom", "wav"), pairs)

    def swap_wav(x, mask):
        return lax.ppermute(x, "wav", [(w, w ^ mask) for w in range(wavs)])

    each = range(CHAINS)
    tables = phase_tables(positions)
    phases_up, arrived = [], []
    for c in each:
        phases, leaving = spectrum_upper(lay, c, inv_atoms, tables, features)
        phases_up.append(phases)
        arrived.append(swap(leaving, c, 0))
    phases_low, kept = spectrum_lower(lay, inv_atoms, tables, features)

    if wavs == 2 and share == HALO_BLK:
        packed = pack_half(positions, features, share)
        count = doms * wavs
        chain = [(g, (g + 1 if g % 2 else g - 1) % count) for g in range(count)]
        halos = [lax.ppermute(packed, ("dom", "wav"), chain)]
    else:
        halos = side_halos(positions, features)
    short = short_range(neighbours, positions, features, halos, message_weight[0], share)

    sums = list(lattice_weights(lay, wavevectors, spectral_filter[0]))
    mask = wavs // 2
    while mask:
        others = [swap_wav(s, mask) for s in sums[mask:]]
        if mask == 1:
            sums = [sums[0], *others]
        else:
            sums = [add_plain(a, b) for a, b in zip(sums[:mask], others)]
        mask //= 2

    for step in range(1, bits - 1):
        for c in each:
            kept[c], leaving = add_split(kept[c], arrived[c])
            arrived[c] = swap(leaving, c, step)
    total, leaving = add_all(kept, arrived)
    filts = list(filtered(total, swap(leaving, 0, bits - 1), spectral_mix[0], sums))
    for step in reversed(range(1, bits - 1)):
        for c in each:
            filts[c] = join(filts[c], swap(filts[c], c, step))
    filts_up = [swap(filts[c], c, 0) for c in each]
    part = back_lower(phases_low, filts)
    for c in range(CHAINS - 1):
        part = back_more(part, phases_up[c], filts_up[c])
    total, leaving = back_last(part, phases_up[-1], filts_up[-1], short, inv_waves)
    mask = wavs // 2
    while mask > 1:
        total = add_plain(total, swap_wav(total, mask))
        leaving = total
        mask //= 2
    return finish(features, total, swap_wav(leaving, 1))


def side_halos(positions, features):
    doms, atoms = lax.axis_size("dom"), features.shape[0]
    rim = HALO_BLK * BLOCK
    up = [(i, (i + 1) % doms) for i in range(doms)]
    down = [(j, i) for i, j in up]
    halos = []
    for at, pairs in ((atoms - rim, up), (0, down)):
        packed = pack_side(positions[:, at : at + rim], features[at : at + rim])
        halos.append(lax.ppermute(packed, "dom", pairs))
    return halos


def pack_side(positions, features):
    rows, channels = features.shape
    extra = -(-9 * HALO_BLK // (2 * TILE)) * 2 * TILE

    def body(pos_ref, h_ref, out_ref):
        out_ref[:rows, :] = h_ref[...]
        fill_coordinates(pos_ref[...], out_ref, rows)

    return call(body, VMEM((rows + extra, channels), BF16), positions, features)


def fill_coordinates(pos, out_ref, rows):
    high = pos.astype(BF16).astype(F32)
    mid = (pos - high).astype(BF16).astype(F32)
    parts = []
    for part in (high, mid, pos - high - mid):
        for axis in range(3):
            for b in range(rows // BLOCK):
                parts.append(part[axis : axis + 1, b * BLOCK : (b + 1) * BLOCK])
    parts += [jnp.zeros_like(parts[0])] * (out_ref.shape[0] - rows - len(parts))
    out_ref[rows:, :] = jnp.concatenate(parts, axis=0).astype(BF16)


def solution(mesh):
    placed = (
        P("dom", None),
        P(None, "dom"),
        P("dom", None),
        P(None, "wav"),
        P(),
        P(),
        P(None, "wav", None),
    )

    return jax.shard_map(local, mesh=mesh, in_specs=placed, out_specs=P("dom", None), check_vma=False)
```

```python
import math

import jax
import jax.numpy as jnp
from jax import lax
from jax.experimental import pallas as pl
from jax.experimental.pallas import tpu as pltpu
from jax.sharding import PartitionSpec as P


KV = 8192
BLOCK = 128
NBR = 8
HALO_BLK = 4
TOP = 8
SPAN = 2 * TOP + 1

TWO_PI = 2.0 * math.pi
KERNEL_DECAY = 12.0
DECAY_LOG2 = -KERNEL_DECAY * math.log2(math.e)
SPLIT = 64
PAIR_SCALE = 1.0 / 16.0

TILE = 8
CHAINS = 2
Q_TILES = 2 * SPAN + 3
Q_ROWS = Q_TILES * TILE
FIRST_TILE = 2 + 2 * TOP
ZERO_TILES = Q_TILES - FIRST_TILE
ALL_TILES = ZERO_TILES + TOP * Q_TILES
assert TOP == TILE

F32 = jnp.float32
BF16 = jnp.bfloat16
VMEM = pltpu.VMEM


def in_vmem(array):
    return pltpu.with_memory_space_constraint(array, VMEM)


def in_hbm(array):
    return pltpu.with_memory_space_constraint(array, pltpu.HBM)


def call(body, out, *args, smem=(), hbm=(), scratch=(), limit=16):
    spec = pl.BlockSpec(memory_space=VMEM)
    specs = [spec] * len(args) + [pl.BlockSpec(memory_space=pltpu.SMEM)] * len(smem)
    specs += [pl.BlockSpec(memory_space=pltpu.HBM)] * len(hbm)
    single = not isinstance(out, (list, tuple))
    return pl.pallas_call(
        body,
        in_specs=specs,
        out_specs=spec if single else [spec] * len(out),
        out_shape=out,
        scratch_shapes=list(scratch),
        compiler_params=pltpu.CompilerParams(vmem_limit_bytes=limit << 20),
    )(*[in_vmem(a) for a in args], *smem, *[in_hbm(a) for a in hbm])


DIVIDE = -(-(1 << 16) // Q_TILES)
assert all((v * DIVIDE) >> 16 == v // Q_TILES for v in range(FIRST_TILE + ALL_TILES))


class Layout:
    def __init__(self, atoms):
        self.atoms = atoms
        self.doms, self.wavs = lax.axis_size("dom"), lax.axis_size("wav")
        self.bits = self.doms.bit_length() - 1
        assert self.doms == 1 << self.bits and self.bits > 3
        assert self.wavs & (self.wavs - 1) == 0
        self.tiles = -(-ALL_TILES // (self.doms * self.wavs * CHAINS))
        self.slice_rows = 2 * TILE * self.tiles
        self.rows = self.slice_rows * self.doms

    def order(self, wav, chain):
        turn = (0, 1, 2, 0)[(CHAINS * wav + chain) % 4]
        first = [0, 1, 2]
        return first[turn:] + first[:turn] + list(range(3, self.bits))

    def code(self, wav, chain):
        dom = lax.axis_index("dom")
        codes = []
        for w in (0, 1):
            code = 0
            for step, bit in enumerate(self.order(w, chain)):
                code = code | (((dom >> bit) & 1) << (self.bits - 1 - step))
            codes.append(code)
        return jnp.where((wav & 1) == 0, codes[0], codes[1])

    def first_tile(self, wav, chain, position):
        number = CHAINS * wav + chain
        return (number * self.doms + (position ^ self.code(wav, chain))) * self.tiles


def tile_place(tile):
    tile = jnp.minimum(tile, ALL_TILES - 1) + FIRST_TILE
    n2 = (tile * DIVIDE) >> 16
    return n2, tile - n2 * Q_TILES


def times(a, b):
    return a[0] * b[0] - a[1] * b[1], a[0] * b[1] + a[1] * b[0]


def fill_tables(pos_ref, xyc_ref, xys_ref, zc_ref, zs_ref):
    angle = TWO_PI * pos_ref[...]
    power = [(jnp.ones_like(angle), jnp.zeros_like(angle)), (jnp.cos(angle), jnp.sin(angle))]
    for n in range(2, TOP + 1):
        power.append(times(power[n // 2], power[n - n // 2]))
    wide = (TILE, angle.shape[1])

    def row(n, axis):
        c, s = power[abs(n)]
        c, s = c[axis : axis + 1, :], s[axis : axis + 1, :]
        return c, (s if n >= 0 else -s)

    def spread(n, axis):
        return tuple(jnp.broadcast_to(v, wide) for v in row(n, axis))

    def stack(numbers, axis):
        rows = [row(n, axis) for n in numbers]
        return tuple(jnp.concatenate([r[i] for r in rows], axis=0) for i in (0, 1))

    for n in range(TOP + 1):
        at = slice(n * TILE, (n + 1) * TILE)
        zc_ref[at, :], zs_ref[at, :] = spread(n, 2)

    def put(tile, a, b):
        at = slice(tile * TILE, (tile + 1) * TILE)
        xyc_ref[at, :], xys_ref[at, :] = times(a, b)

    below, above = stack(range(-TOP, 0), 1), stack(range(TOP), 1)
    edge = spread(TOP, 1)
    for n in range(-TOP, TOP + 1):
        here = spread(n, 0)
        put(1 + 2 * (n + TOP), here, below)
        put(2 + 2 * (n + TOP), here, above)
    put(0, stack(range(-TOP, 0), 0), edge)
    put(Q_TILES - 2, stack(range(TOP), 0), edge)
    put(Q_TILES - 1, spread(TOP, 0), edge)


def fill_phases(lay, chain, low, count, tables, h_ref, p_ref, p_at, put):
    xyc_ref, xys_ref, zc_ref, zs_ref = tables
    wav = lax.axis_index("wav")
    group = max(1, count // 2)
    rows = group * lay.slice_rows
    feats = h_ref[...]

    for step in range(count // group):
        start = p_at + step * rows
        for part in range(group):
            base = lay.first_tile(wav, chain, low + step * group + part)
            for i in range(lay.tiles):
                n2, qt = tile_place(base + i)
                q_at = pl.ds(pl.multiple_of(qt * TILE, TILE), TILE)
                z_at = pl.ds(pl.multiple_of(n2 * TILE, TILE), TILE)
                c, s = times((xyc_ref[q_at, :], xys_ref[q_at, :]), (zc_ref[z_at, :], zs_ref[z_at, :]))
                at = start + (part * lay.tiles + i) * 2 * TILE
                p_ref[at : at + 2 * TILE, :] = jnp.concatenate([c, s], axis=0).astype(BF16)
        here = slice(start, start + rows)
        at = slice(step * rows, (step + 1) * rows)
        put(at, jnp.dot(p_ref[here, :], feats, preferred_element_type=F32))


def phase_tables(positions, features):
    atoms = positions.shape[1]
    table = [(Q_ROWS, atoms)] * 2 + [((TOP + 1) * TILE, atoms)] * 2

    def body(pos_hbm, h_hbm, *refs):
        *table_refs, pos_ref, h_ref, sems = refs
        bring_pos = pltpu.make_async_copy(pos_hbm, pos_ref, sems.at[0])
        bring_h = pltpu.make_async_copy(h_hbm, h_ref, sems.at[1])
        bring_pos.start()
        bring_h.start()
        bring_pos.wait()
        fill_tables(pos_ref, *table_refs)
        bring_h.wait()

    out = [VMEM(shape, F32) for shape in table]
    out += [VMEM(positions.shape, F32), VMEM(features.shape, BF16)]
    *tables, pos, h = call(
        body, out, hbm=[positions, features],
        scratch=[pltpu.SemaphoreType.DMA((2,))],
    )
    return tables, pos, h


def spectrum_upper(lay, chain, scale, tables, features):
    half = lay.doms // 2

    def body(xyc, xys, zc, zs, h_ref, p_ref, s_ref):
        def put(at, value):
            s_ref[at, :] = (value * scale).astype(BF16)

        fill_phases(lay, chain, half, half, (xyc, xys, zc, zs), h_ref, p_ref, 0, put)

    out = [VMEM((lay.rows // 2, lay.atoms), BF16), VMEM((lay.rows // 2, features.shape[1]), BF16)]
    return call(body, out, *tables, features)


def spectrum_lower(lay, scale, tables, features):
    def body(xyc, xys, zc, zs, h_ref, p_ref, *s_refs):
        for chain, s_ref in enumerate(s_refs):

            def put(at, value):
                s_ref[at, :] = value * scale

            fill_phases(
                lay, chain, 0, lay.doms // 2, (xyc, xys, zc, zs), h_ref, p_ref,
                chain * (lay.rows // 2), put,
            )

    out = [VMEM((CHAINS * lay.rows // 2, lay.atoms), BF16)]
    out += [VMEM((lay.rows // 2, features.shape[1]), F32)] * CHAINS
    phases, *sums = call(body, out, *tables, features)
    return phases, sums


def lattice_weights(lay, wavevectors, weights):
    waves, channels = weights.shape
    tiles = 2 * lay.tiles * lay.wavs * CHAINS
    chunk = min(waves, 1024)

    def body(wave_ref, filter_ref, *refs):
        *out_refs, hot_ref = refs
        wav = lax.axis_index("wav")
        bases = []
        for v in range(lay.wavs):
            for chain in range(CHAINS):
                for p in range(2):
                    first = lay.first_tile(wav ^ v, chain, p)
                    for i in range(lay.tiles):
                        n2, qt = tile_place(first + i)
                        base = n2 * Q_ROWS + qt * TILE
                        bases.append(jnp.where(first + i < ALL_TILES, base, -Q_ROWS))
        total = None
        for start in range(0, waves, chunk):
            at = slice(start, start + chunk)
            n0, n1, n2 = (wave_ref[a : a + 1, at] for a in range(3))
            negative = jnp.logical_or(n0 < 0, jnp.logical_and(n0 == 0, n1 < 0))
            flip = jnp.logical_or(n2 < 0, jnp.logical_and(n2 == 0, negative))
            n0, n1, n2 = (jnp.where(flip, -n, n) for n in (n0, n1, n2))
            inner = TILE + (n0 + TOP) * 2 * TILE + n1 + TOP
            outer = jnp.where(n0 < 0, n0 + TOP, (Q_TILES - 2) * TILE + n0)
            key = n2 * Q_ROWS + jnp.where(n1 == TOP, outer, inner)
            wide = jnp.broadcast_to(key, (TILE, chunk))
            shifted = wide - lax.broadcasted_iota(jnp.int32, wide.shape, 0)
            for t in range(0, tiles, 2):
                both = [jnp.where(shifted == bases[u], 1.0, 0.0) for u in (t, t + 1)]
                hot_ref[t * TILE : (t + 2) * TILE, :] = jnp.concatenate(both, axis=0).astype(BF16)
            w = filter_ref[at, :]
            high = w.astype(BF16)
            low = (w - high.astype(F32)).astype(BF16)
            part = jnp.dot(
                hot_ref[...], jnp.concatenate([high, low], axis=1), preferred_element_type=F32
            )
            total = part if total is None else total + part
        total = total[:, :channels] + total[:, channels:]
        rows = tiles * TILE // lay.wavs
        for v, ref in enumerate(out_refs):
            ref[...] = total[v * rows : (v + 1) * rows]

    out = [VMEM((tiles * TILE // lay.wavs, channels), F32)] * lay.wavs
    return call(
        body, out, wavevectors, weights,
        scratch=[VMEM((tiles * TILE, chunk), BF16)],
    )


def add_split(mine, other):
    rows, channels = mine.shape

    def body(a_ref, b_ref, keep_ref, send_ref):
        total = a_ref[...] + b_ref[...].astype(F32)
        keep_ref[...] = total[: rows // 2]
        send_ref[...] = total[rows // 2 :].astype(BF16)

    out = [VMEM((rows // 2, channels), F32), VMEM((rows // 2, channels), BF16)]
    return call(body, out, mine, other)


def add_all(mine, others):
    rows, channels = mine[0].shape

    def body(*refs):
        keep_ref, send_ref = refs[-2:]
        for i in range(CHAINS):
            at = slice(i * rows, (i + 1) * rows)
            total = refs[i][...] + refs[CHAINS + i][...].astype(F32)
            keep_ref[at, :] = total
            send_ref[at, :] = total.astype(BF16)

    out = [VMEM((CHAINS * rows, channels), t) for t in (F32, BF16)]
    return call(body, out, *mine, *others)


def add_plain(mine, other):
    def body(a_ref, b_ref, out_ref):
        out_ref[...] = a_ref[...] + b_ref[...].astype(F32)

    return call(body, VMEM(mine.shape, F32), mine, other)


def dot_exact(a, b):
    return jnp.dot(a, b, precision=lax.Precision.HIGHEST, preferred_element_type=F32)


def filtered(mine, other, mixing, weights):
    rows, channels = mine.shape
    part = rows // CHAINS
    groups = rows // (2 * TILE)

    def body(mine_ref, other_ref, mix_ref, *refs):
        weight_refs, out_refs = refs[:-CHAINS], refs[-CHAINS:]
        there = other_ref[...].astype(F32)
        cuts = [there[i * part // 2 : (i + 1) * part // 2] for i in range(2 * CHAINS)]
        there = jnp.concatenate([cuts[i ^ 1] for i in range(2 * CHAINS)], axis=0)
        mixed = dot_exact(mine_ref[...] + there, mix_ref[...])
        factor = weight_refs[0][...]
        for ref in weight_refs[1:]:
            factor = factor + ref[...]
        mixed = mixed.reshape(groups, 2, TILE, channels) * factor.reshape(groups, 1, TILE, channels)
        mixed = mixed.reshape(rows, channels).astype(BF16)
        for i, ref in enumerate(out_refs):
            ref[...] = mixed[i * part : (i + 1) * part]

    out = [VMEM((part, channels), BF16)] * CHAINS
    return call(body, out, mine, other, mixing, *weights)


def join(low, high):
    def body(a_ref, b_ref, out_ref):
        rows = a_ref.shape[0]
        out_ref[:rows, :] = a_ref[...]
        out_ref[rows:, :] = b_ref[...]

    out = VMEM((low.shape[0] + high.shape[0], low.shape[1]), low.dtype)
    return call(body, out, low, high)


def pack_half(positions, features, share):
    rows, channels = share * BLOCK, features.shape[1]
    extra = -(-9 * share // (2 * TILE)) * 2 * TILE

    def body(pos_ref, h_ref, out_ref):
        start = pl.multiple_of(lax.axis_index("wav") * rows, rows)
        out_ref[:rows, :] = h_ref[pl.ds(start, rows), :]
        fill_coordinates(pos_ref[:, pl.ds(start, rows)], out_ref, rows)

    return call(body, VMEM((rows + extra, channels), BF16), positions, features)


def short_range(neighbours, positions, features, halos, weight, share):
    channels = features.shape[1]
    own = features.shape[0] // BLOCK
    near = [HALO_BLK] * len(halos)
    blocks = own + sum(near)
    both = len(halos) == 2

    def body(pos_ref, h_ref, weight_ref, *refs):
        halo_refs, (lists, out_ref, val_ref, at_ref) = refs[: len(halos)], refs[len(halos) :]
        w = weight_ref[...]

        def project(rows):
            return jnp.dot(rows, w, preferred_element_type=F32).astype(BF16)

        val_ref[: own * BLOCK, :] = project(h_ref[...])
        pos = pos_ref[...]
        for b in range(own):
            at_ref[b, 0:3, :] = pos[:, b * BLOCK : (b + 1) * BLOCK]
        at = own
        for ref, count in zip(halo_refs, near):
            rows = count * BLOCK
            val_ref[at * BLOCK : (at + count) * BLOCK, :] = project(ref[:rows, :])
            pieces = ref[rows:, :].astype(F32)
            n = 3 * count
            there = pieces[:n] + pieces[n : 2 * n] + pieces[2 * n : 3 * n]
            for b in range(count):
                for axis in range(3):
                    k = axis * count + b
                    at_ref[at + b, axis : axis + 1, :] = there[k : k + 1]
            at += count
        first = lax.axis_index("wav") * share

        def block(b, carry):
            columns = jnp.transpose(at_ref[first + b])
            total = jnp.zeros((BLOCK, channels), F32)
            for m in range(NBR):
                ext = lists[first + b, m]
                inside = jnp.logical_and(ext >= HALO_BLK, ext < HALO_BLK + own)
                if both:
                    outside = own + jnp.where(ext < HALO_BLK, ext, ext - own)
                else:
                    outside = own + jnp.where(ext < HALO_BLK, ext, ext - HALO_BLK - own)
                sender = jnp.where(inside, ext - HALO_BLK, outside)
                sent = at_ref[sender]
                parts = []
                for low in range(0, BLOCK, SPLIT):
                    distance = None
                    for axis in range(3):
                        here = columns[low : low + SPLIT, axis : axis + 1]
                        delta = here - sent[axis : axis + 1, :]
                        delta = delta - jnp.round(delta)
                        square = delta * delta
                        distance = square if distance is None else distance + square
                    parts.append(jnp.exp2(distance * DECAY_LOG2).astype(BF16))
                kernel = jnp.concatenate(parts, axis=0)
                rows = pl.ds(pl.multiple_of(sender * BLOCK, BLOCK), BLOCK)
                total = total + jnp.dot(kernel, val_ref[rows, :], preferred_element_type=F32)
            out_ref[pl.ds(pl.multiple_of(b * BLOCK, BLOCK), BLOCK), :] = total * PAIR_SCALE
            return carry

        lax.fori_loop(0, share, block, 0, unroll=True)

    return call(
        body, VMEM((share * BLOCK, channels), F32), positions, features, weight,
        *halos, smem=[neighbours],
        scratch=[VMEM((blocks * BLOCK, channels), BF16), VMEM((blocks, TILE, BLOCK), F32)],
    )


def transposed_dot(phases, filt):
    dims = (((0,), (0,)), ((), ()))
    return lax.dot_general(phases, filt, dims, preferred_element_type=F32)


def back_lower(phases, filts):
    def body(p_ref, *refs):
        *f_refs, out_ref = refs
        filt = jnp.concatenate([ref[...] for ref in f_refs], axis=0)
        out_ref[...] = transposed_dot(p_ref[...], filt)

    out = VMEM((phases.shape[1], filts[0].shape[1]), F32)
    return call(body, out, phases, *filts)


def back_more(part, phases, filt):
    def body(part_ref, p_ref, f_ref, out_ref):
        out_ref[...] = part_ref[...] + transposed_dot(p_ref[...], f_ref[...])

    return call(body, VMEM(part.shape, F32), part, phases, filt)


def back_last(part, phases, filt, short, scale):
    rows = short.shape[0]

    def body(part_ref, p_ref, f_ref, short_ref, out_ref, send_ref):
        out_ref[...] = (part_ref[...] + transposed_dot(p_ref[...], f_ref[...])) * scale
        here = pl.ds(pl.multiple_of(lax.axis_index("wav") * rows, rows), rows)
        out_ref[here, :] += short_ref[...]
        send_ref[...] = out_ref[...].astype(BF16)

    out = [VMEM(part.shape, t) for t in (F32, BF16)]
    return call(body, out, part, phases, filt, short)


def finish(features, total, other):
    def body(h_ref, a_ref, b_ref, out_ref):
        total = a_ref[...] + b_ref[...].astype(F32)
        out_ref[...] = (h_ref[...].astype(F32) + total * jax.nn.sigmoid(total)).astype(BF16)

    out = jax.ShapeDtypeStruct(features.shape, BF16)
    return call(body, out, features, total, other)


def local(
    node_features, positions, neighbours, wavevectors, message_weight, spectral_mix, spectral_filter
):
    features = node_features
    atoms = features.shape[0]
    lay = Layout(atoms)
    doms, wavs, bits = lay.doms, lay.wavs, lay.bits
    blocks = atoms // BLOCK
    share = blocks // wavs
    inv_atoms = 1.0 / math.sqrt(atoms * doms)
    inv_waves = 1.0 / math.sqrt(KV)

    def swap(x, chain, step):
        pairs = []
        for d in range(doms):
            for w in range(wavs):
                pairs.append((d * wavs + w, (d ^ (1 << lay.order(w, chain)[step])) * wavs + w))
        return lax.ppermute(x, ("dom", "wav"), pairs)

    def swap_wav(x, mask):
        return lax.ppermute(x, "wav", [(w, w ^ mask) for w in range(wavs)])

    each = range(CHAINS)
    tables, positions, features = phase_tables(positions, features)
    phases_up, arrived = [], []
    for c in each:
        phases, leaving = spectrum_upper(lay, c, inv_atoms, tables, features)
        phases_up.append(phases)
        arrived.append(swap(leaving, c, 0))
    phases_low, kept = spectrum_lower(lay, inv_atoms, tables, features)

    if wavs == 2 and share == HALO_BLK:
        packed = pack_half(positions, features, share)
        count = doms * wavs
        chain = [(g, (g + 1 if g % 2 else g - 1) % count) for g in range(count)]
        halos = [lax.ppermute(packed, ("dom", "wav"), chain)]
    else:
        halos = side_halos(positions, features)
    short = short_range(neighbours, positions, features, halos, message_weight[0], share)

    sums = list(lattice_weights(lay, wavevectors, spectral_filter[0]))
    mask = wavs // 2
    while mask:
        others = [swap_wav(s, mask) for s in sums[mask:]]
        if mask == 1:
            sums = [sums[0], *others]
        else:
            sums = [add_plain(a, b) for a, b in zip(sums[:mask], others)]
        mask //= 2

    for step in range(1, bits - 1):
        for c in each:
            kept[c], leaving = add_split(kept[c], arrived[c])
            arrived[c] = swap(leaving, c, step)
    total, leaving = add_all(kept, arrived)
    filts = list(filtered(total, swap(leaving, 0, bits - 1), spectral_mix[0], sums))
    for step in reversed(range(1, bits - 1)):
        for c in each:
            filts[c] = join(filts[c], swap(filts[c], c, step))
    filts_up = [swap(filts[c], c, 0) for c in each]
    part = back_lower(phases_low, filts)
    for c in range(CHAINS - 1):
        part = back_more(part, phases_up[c], filts_up[c])
    total, leaving = back_last(part, phases_up[-1], filts_up[-1], short, inv_waves)
    mask = wavs // 2
    while mask > 1:
        total = add_plain(total, swap_wav(total, mask))
        leaving = total
        mask //= 2
    return finish(features, total, swap_wav(leaving, 1))


def side_halos(positions, features):
    doms, atoms = lax.axis_size("dom"), features.shape[0]
    rim = HALO_BLK * BLOCK
    up = [(i, (i + 1) % doms) for i in range(doms)]
    down = [(j, i) for i, j in up]
    halos = []
    for at, pairs in ((atoms - rim, up), (0, down)):
        packed = pack_side(positions[:, at : at + rim], features[at : at + rim])
        halos.append(lax.ppermute(packed, "dom", pairs))
    return halos


def pack_side(positions, features):
    rows, channels = features.shape
    extra = -(-9 * HALO_BLK // (2 * TILE)) * 2 * TILE

    def body(pos_ref, h_ref, out_ref):
        out_ref[:rows, :] = h_ref[...]
        fill_coordinates(pos_ref[...], out_ref, rows)

    return call(body, VMEM((rows + extra, channels), BF16), positions, features)


def fill_coordinates(pos, out_ref, rows):
    high = pos.astype(BF16).astype(F32)
    mid = (pos - high).astype(BF16).astype(F32)
    parts = []
    for part in (high, mid, pos - high - mid):
        for axis in range(3):
            for b in range(rows // BLOCK):
                parts.append(part[axis : axis + 1, b * BLOCK : (b + 1) * BLOCK])
    parts += [jnp.zeros_like(parts[0])] * (out_ref.shape[0] - rows - len(parts))
    out_ref[rows:, :] = jnp.concatenate(parts, axis=0).astype(BF16)


def solution(mesh):
    placed = (
        P("dom", None),
        P(None, "dom"),
        P("dom", None),
        P(None, "wav"),
        P(),
        P(),
        P(None, "wav", None),
    )

    return jax.shard_map(local, mesh=mesh, in_specs=placed, out_specs=P("dom", None), check_vma=False)
```

```python
import math

import jax
import jax.numpy as jnp
from jax import lax
from jax.experimental import pallas as pl
from jax.experimental.pallas import tpu as pltpu
from jax.sharding import PartitionSpec as P


KV = 8192
BLOCK = 128
NBR = 8
HALO_BLK = 4
TOP = 8
SPAN = 2 * TOP + 1

TWO_PI = 2.0 * math.pi
KERNEL_DECAY = 12.0
DECAY_LOG2 = -KERNEL_DECAY * math.log2(math.e)
SPLIT = 64
PAIR_SCALE = 1.0 / 16.0

TILE = 8
CHAINS = 2
Q_TILES = 2 * SPAN + 3
Q_ROWS = Q_TILES * TILE
FIRST_TILE = 2 + 2 * TOP
ZERO_TILES = Q_TILES - FIRST_TILE
ALL_TILES = ZERO_TILES + TOP * Q_TILES
assert TOP == TILE

F32 = jnp.float32
BF16 = jnp.bfloat16
VMEM = pltpu.VMEM


def in_vmem(array):
    return pltpu.with_memory_space_constraint(array, VMEM)


def in_hbm(array):
    return pltpu.with_memory_space_constraint(array, pltpu.HBM)


def call(body, out, *args, smem=(), hbm=(), scratch=(), limit=16):
    spec = pl.BlockSpec(memory_space=VMEM)
    specs = [spec] * len(args) + [pl.BlockSpec(memory_space=pltpu.SMEM)] * len(smem)
    specs += [pl.BlockSpec(memory_space=pltpu.HBM)] * len(hbm)
    single = not isinstance(out, (list, tuple))
    return pl.pallas_call(
        body,
        in_specs=specs,
        out_specs=spec if single else [spec] * len(out),
        out_shape=out,
        scratch_shapes=list(scratch),
        compiler_params=pltpu.CompilerParams(vmem_limit_bytes=limit << 20),
    )(*[in_vmem(a) for a in args], *smem, *[in_hbm(a) for a in hbm])


DIVIDE = -(-(1 << 16) // Q_TILES)
assert all((v * DIVIDE) >> 16 == v // Q_TILES for v in range(FIRST_TILE + ALL_TILES))


class Layout:
    def __init__(self, atoms):
        self.atoms = atoms
        self.doms, self.wavs = lax.axis_size("dom"), lax.axis_size("wav")
        self.bits = self.doms.bit_length() - 1
        assert self.doms == 1 << self.bits and self.bits > 3
        assert self.wavs & (self.wavs - 1) == 0
        self.tiles = -(-ALL_TILES // (self.doms * self.wavs * CHAINS))
        self.slice_rows = 2 * TILE * self.tiles
        self.rows = self.slice_rows * self.doms

    def order(self, wav, chain):
        turn = (2, 0, 0, 1)[(CHAINS * wav + chain) % 4]
        first = [0, 1, 2]
        return first[turn:] + first[:turn] + list(range(3, self.bits))

    def code(self, wav, chain):
        dom = lax.axis_index("dom")
        codes = []
        for w in (0, 1):
            code = 0
            for step, bit in enumerate(self.order(w, chain)):
                code = code | (((dom >> bit) & 1) << (self.bits - 1 - step))
            codes.append(code)
        return jnp.where((wav & 1) == 0, codes[0], codes[1])

    def first_tile(self, wav, chain, position):
        number = CHAINS * wav + chain
        return (number * self.doms + (position ^ self.code(wav, chain))) * self.tiles


def tile_place(tile):
    tile = jnp.minimum(tile, ALL_TILES - 1) + FIRST_TILE
    n2 = (tile * DIVIDE) >> 16
    return n2, tile - n2 * Q_TILES


def times(a, b):
    return a[0] * b[0] - a[1] * b[1], a[0] * b[1] + a[1] * b[0]


def fill_tables(pos_ref, xyc_ref, xys_ref, zc_ref, zs_ref):
    angle = TWO_PI * pos_ref[...]
    power = [(jnp.ones_like(angle), jnp.zeros_like(angle)), (jnp.cos(angle), jnp.sin(angle))]
    for n in range(2, TOP + 1):
        power.append(times(power[n // 2], power[n - n // 2]))
    wide = (TILE, angle.shape[1])

    def row(n, axis):
        c, s = power[abs(n)]
        c, s = c[axis : axis + 1, :], s[axis : axis + 1, :]
        return c, (s if n >= 0 else -s)

    def spread(n, axis):
        return tuple(jnp.broadcast_to(v, wide) for v in row(n, axis))

    def stack(numbers, axis):
        rows = [row(n, axis) for n in numbers]
        return tuple(jnp.concatenate([r[i] for r in rows], axis=0) for i in (0, 1))

    for n in range(TOP + 1):
        at = slice(n * TILE, (n + 1) * TILE)
        zc_ref[at, :], zs_ref[at, :] = spread(n, 2)

    def put(tile, a, b):
        at = slice(tile * TILE, (tile + 1) * TILE)
        xyc_ref[at, :], xys_ref[at, :] = times(a, b)

    below, above = stack(range(-TOP, 0), 1), stack(range(TOP), 1)
    edge = spread(TOP, 1)
    for n in range(-TOP, TOP + 1):
        here = spread(n, 0)
        put(1 + 2 * (n + TOP), here, below)
        put(2 + 2 * (n + TOP), here, above)
    put(0, stack(range(-TOP, 0), 0), edge)
    put(Q_TILES - 2, stack(range(TOP), 0), edge)
    put(Q_TILES - 1, spread(TOP, 0), edge)


def fill_phases(lay, chain, low, count, tables, h_ref, p_ref, p_at, put):
    xyc_ref, xys_ref, zc_ref, zs_ref = tables
    wav = lax.axis_index("wav")
    group = max(1, count // 2)
    rows = group * lay.slice_rows
    feats = h_ref[...]

    for step in range(count // group):
        start = p_at + step * rows
        for part in range(group):
            base = lay.first_tile(wav, chain, low + step * group + part)
            for i in range(lay.tiles):
                n2, qt = tile_place(base + i)
                q_at = pl.ds(pl.multiple_of(qt * TILE, TILE), TILE)
                z_at = pl.ds(pl.multiple_of(n2 * TILE, TILE), TILE)
                c, s = times((xyc_ref[q_at, :], xys_ref[q_at, :]), (zc_ref[z_at, :], zs_ref[z_at, :]))
                at = start + (part * lay.tiles + i) * 2 * TILE
                p_ref[at : at + 2 * TILE, :] = jnp.concatenate([c, s], axis=0).astype(BF16)
        here = slice(start, start + rows)
        at = slice(step * rows, (step + 1) * rows)
        put(at, jnp.dot(p_ref[here, :], feats, preferred_element_type=F32))


def phase_tables(positions, features):
    atoms = positions.shape[1]
    table = [(Q_ROWS, atoms)] * 2 + [((TOP + 1) * TILE, atoms)] * 2

    def body(pos_hbm, h_hbm, *refs):
        *table_refs, pos_ref, h_ref, sems = refs
        bring_pos = pltpu.make_async_copy(pos_hbm, pos_ref, sems.at[0])
        bring_h = pltpu.make_async_copy(h_hbm, h_ref, sems.at[1])
        bring_pos.start()
        bring_h.start()
        bring_pos.wait()
        fill_tables(pos_ref, *table_refs)
        bring_h.wait()

    out = [VMEM(shape, F32) for shape in table]
    out += [VMEM(positions.shape, F32), VMEM(features.shape, BF16)]
    *tables, pos, h = call(
        body, out, hbm=[positions, features],
        scratch=[pltpu.SemaphoreType.DMA((2,))],
    )
    return tables, pos, h


def spectrum_upper(lay, chain, scale, tables, features):
    half = lay.doms // 2

    def body(xyc, xys, zc, zs, h_ref, p_ref, s_ref):
        def put(at, value):
            s_ref[at, :] = (value * scale).astype(BF16)

        fill_phases(lay, chain, half, half, (xyc, xys, zc, zs), h_ref, p_ref, 0, put)

    out = [VMEM((lay.rows // 2, lay.atoms), BF16), VMEM((lay.rows // 2, features.shape[1]), BF16)]
    return call(body, out, *tables, features)


def spectrum_lower(lay, scale, tables, features):
    def body(xyc, xys, zc, zs, h_ref, p_ref, *s_refs):
        for chain, s_ref in enumerate(s_refs):

            def put(at, value):
                s_ref[at, :] = value * scale

            fill_phases(
                lay, chain, 0, lay.doms // 2, (xyc, xys, zc, zs), h_ref, p_ref,
                chain * (lay.rows // 2), put,
            )

    out = [VMEM((CHAINS * lay.rows // 2, lay.atoms), BF16)]
    out += [VMEM((lay.rows // 2, features.shape[1]), F32)] * CHAINS
    phases, *sums = call(body, out, *tables, features)
    return phases, sums


def lattice_weights(lay, wavevectors, weights):
    waves, channels = weights.shape
    tiles = 2 * lay.tiles * lay.wavs * CHAINS
    chunk = min(waves, 1024)

    def body(wave_ref, filter_ref, *refs):
        *out_refs, hot_ref = refs
        wav = lax.axis_index("wav")
        bases = []
        for v in range(lay.wavs):
            for chain in range(CHAINS):
                for p in range(2):
                    first = lay.first_tile(wav ^ v, chain, p)
                    for i in range(lay.tiles):
                        n2, qt = tile_place(first + i)
                        base = n2 * Q_ROWS + qt * TILE
                        bases.append(jnp.where(first + i < ALL_TILES, base, -Q_ROWS))
        total = None
        for start in range(0, waves, chunk):
            at = slice(start, start + chunk)
            n0, n1, n2 = (wave_ref[a : a + 1, at] for a in range(3))
            negative = jnp.logical_or(n0 < 0, jnp.logical_and(n0 == 0, n1 < 0))
            flip = jnp.logical_or(n2 < 0, jnp.logical_and(n2 == 0, negative))
            n0, n1, n2 = (jnp.where(flip, -n, n) for n in (n0, n1, n2))
            inner = TILE + (n0 + TOP) * 2 * TILE + n1 + TOP
            outer = jnp.where(n0 < 0, n0 + TOP, (Q_TILES - 2) * TILE + n0)
            key = n2 * Q_ROWS + jnp.where(n1 == TOP, outer, inner)
            wide = jnp.broadcast_to(key, (TILE, chunk))
            shifted = wide - lax.broadcasted_iota(jnp.int32, wide.shape, 0)
            for t in range(0, tiles, 2):
                both = [jnp.where(shifted == bases[u], 1.0, 0.0) for u in (t, t + 1)]
                hot_ref[t * TILE : (t + 2) * TILE, :] = jnp.concatenate(both, axis=0).astype(BF16)
            w = filter_ref[at, :]
            high = w.astype(BF16)
            low = (w - high.astype(F32)).astype(BF16)
            part = jnp.dot(
                hot_ref[...], jnp.concatenate([high, low], axis=1), preferred_element_type=F32
            )
            total = part if total is None else total + part
        total = total[:, :channels] + total[:, channels:]
        rows = tiles * TILE // lay.wavs
        for v, ref in enumerate(out_refs):
            ref[...] = total[v * rows : (v + 1) * rows]

    out = [VMEM((tiles * TILE // lay.wavs, channels), F32)] * lay.wavs
    return call(
        body, out, wavevectors, weights,
        scratch=[VMEM((tiles * TILE, chunk), BF16)],
    )


def add_split(mine, other):
    rows, channels = mine.shape

    def body(a_ref, b_ref, keep_ref, send_ref):
        total = a_ref[...] + b_ref[...].astype(F32)
        keep_ref[...] = total[: rows // 2]
        send_ref[...] = total[rows // 2 :].astype(BF16)

    out = [VMEM((rows // 2, channels), F32), VMEM((rows // 2, channels), BF16)]
    return call(body, out, mine, other)


def add_both(mine, other):
    def body(a_ref, b_ref, keep_ref, send_ref):
        total = a_ref[...] + b_ref[...].astype(F32)
        keep_ref[...] = total
        send_ref[...] = total.astype(BF16)

    return call(body, [VMEM(mine.shape, t) for t in (F32, BF16)], mine, other)


def add_plain(mine, other):
    def body(a_ref, b_ref, out_ref):
        out_ref[...] = a_ref[...] + b_ref[...].astype(F32)

    return call(body, VMEM(mine.shape, F32), mine, other)


def dot_exact(a, b):
    return jnp.dot(a, b, precision=lax.Precision.HIGHEST, preferred_element_type=F32)


def filtered(chain, mine, other, mixing, weights):
    rows, channels = mine.shape
    half = rows // 2
    groups = rows // (2 * TILE)

    def body(mine_ref, other_ref, mix_ref, *refs):
        *weight_refs, out_ref = refs
        there = other_ref[...].astype(F32)
        total = mine_ref[...] + jnp.concatenate([there[half:], there[:half]], axis=0)
        mixed = dot_exact(total, mix_ref[...])
        at = slice(chain * half, (chain + 1) * half)
        factor = weight_refs[0][at, :]
        for ref in weight_refs[1:]:
            factor = factor + ref[at, :]
        mixed = mixed.reshape(groups, 2, TILE, channels) * factor.reshape(groups, 1, TILE, channels)
        out_ref[...] = mixed.reshape(rows, channels).astype(BF16)

    return call(body, VMEM(mine.shape, BF16), mine, other, mixing, *weights)


def join(low, high):
    def body(a_ref, b_ref, out_ref):
        rows = a_ref.shape[0]
        out_ref[:rows, :] = a_ref[...]
        out_ref[rows:, :] = b_ref[...]

    out = VMEM((low.shape[0] + high.shape[0], low.shape[1]), low.dtype)
    return call(body, out, low, high)


def pack_half(positions, features, share):
    rows, channels = share * BLOCK, features.shape[1]
    extra = -(-9 * share // (2 * TILE)) * 2 * TILE

    def body(pos_ref, h_ref, out_ref):
        start = pl.multiple_of(lax.axis_index("wav") * rows, rows)
        out_ref[:rows, :] = h_ref[pl.ds(start, rows), :]
        fill_coordinates(pos_ref[:, pl.ds(start, rows)], out_ref, rows)

    return call(body, VMEM((rows + extra, channels), BF16), positions, features)


def short_range(neighbours, positions, features, halos, weight, share):
    channels = features.shape[1]
    own = features.shape[0] // BLOCK
    near = [HALO_BLK] * len(halos)
    blocks = own + sum(near)
    both = len(halos) == 2

    def body(pos_ref, h_ref, weight_ref, *refs):
        halo_refs, (lists, out_ref, val_ref, at_ref) = refs[: len(halos)], refs[len(halos) :]
        w = weight_ref[...]

        def project(rows):
            return jnp.dot(rows, w, preferred_element_type=F32).astype(BF16)

        val_ref[: own * BLOCK, :] = project(h_ref[...])
        pos = pos_ref[...]
        for b in range(own):
            at_ref[b, 0:3, :] = pos[:, b * BLOCK : (b + 1) * BLOCK]
        at = own
        for ref, count in zip(halo_refs, near):
            rows = count * BLOCK
            val_ref[at * BLOCK : (at + count) * BLOCK, :] = project(ref[:rows, :])
            pieces = ref[rows:, :].astype(F32)
            n = 3 * count
            there = pieces[:n] + pieces[n : 2 * n] + pieces[2 * n : 3 * n]
            for b in range(count):
                for axis in range(3):
                    k = axis * count + b
                    at_ref[at + b, axis : axis + 1, :] = there[k : k + 1]
            at += count
        first = lax.axis_index("wav") * share

        def block(b, carry):
            columns = jnp.transpose(at_ref[first + b])
            total = jnp.zeros((BLOCK, channels), F32)
            for m in range(NBR):
                ext = lists[first + b, m]
                inside = jnp.logical_and(ext >= HALO_BLK, ext < HALO_BLK + own)
                if both:
                    outside = own + jnp.where(ext < HALO_BLK, ext, ext - own)
                else:
                    outside = own + jnp.where(ext < HALO_BLK, ext, ext - HALO_BLK - own)
                sender = jnp.where(inside, ext - HALO_BLK, outside)
                sent = at_ref[sender]
                parts = []
                for low in range(0, BLOCK, SPLIT):
                    distance = None
                    for axis in range(3):
                        here = columns[low : low + SPLIT, axis : axis + 1]
                        delta = here - sent[axis : axis + 1, :]
                        delta = delta - jnp.round(delta)
                        square = delta * delta
                        distance = square if distance is None else distance + square
                    parts.append(jnp.exp2(distance * DECAY_LOG2).astype(BF16))
                kernel = jnp.concatenate(parts, axis=0)
                rows = pl.ds(pl.multiple_of(sender * BLOCK, BLOCK), BLOCK)
                total = total + jnp.dot(kernel, val_ref[rows, :], preferred_element_type=F32)
            out_ref[pl.ds(pl.multiple_of(b * BLOCK, BLOCK), BLOCK), :] = total * PAIR_SCALE
            return carry

        lax.fori_loop(0, share, block, 0, unroll=True)

    return call(
        body, VMEM((share * BLOCK, channels), F32), positions, features, weight,
        *halos, smem=[neighbours],
        scratch=[VMEM((blocks * BLOCK, channels), BF16), VMEM((blocks, TILE, BLOCK), F32)],
    )


def transposed_dot(phases, filt):
    dims = (((0,), (0,)), ((), ()))
    return lax.dot_general(phases, filt, dims, preferred_element_type=F32)


def back_lower(phases, filts):
    def body(p_ref, *refs):
        *f_refs, out_ref = refs
        filt = jnp.concatenate([ref[...] for ref in f_refs], axis=0)
        out_ref[...] = transposed_dot(p_ref[...], filt)

    out = VMEM((phases.shape[1], filts[0].shape[1]), F32)
    return call(body, out, phases, *filts)


def back_more(part, phases, filt):
    def body(part_ref, p_ref, f_ref, out_ref):
        out_ref[...] = part_ref[...] + transposed_dot(p_ref[...], f_ref[...])

    return call(body, VMEM(part.shape, F32), part, phases, filt)


def back_last(part, phases, filt, short, scale):
    rows = short.shape[0]

    def body(part_ref, p_ref, f_ref, short_ref, out_ref, send_ref):
        out_ref[...] = (part_ref[...] + transposed_dot(p_ref[...], f_ref[...])) * scale
        here = pl.ds(pl.multiple_of(lax.axis_index("wav") * rows, rows), rows)
        out_ref[here, :] += short_ref[...]
        send_ref[...] = out_ref[...].astype(BF16)

    out = [VMEM(part.shape, t) for t in (F32, BF16)]
    return call(body, out, part, phases, filt, short)


def finish(features, total, other):
    def body(h_ref, a_ref, b_ref, out_ref):
        total = a_ref[...] + b_ref[...].astype(F32)
        out_ref[...] = (h_ref[...].astype(F32) + total * jax.nn.sigmoid(total)).astype(BF16)

    out = jax.ShapeDtypeStruct(features.shape, BF16)
    return call(body, out, features, total, other)


def local(
    node_features, positions, neighbours, wavevectors, message_weight, spectral_mix, spectral_filter
):
    features = node_features
    atoms = features.shape[0]
    lay = Layout(atoms)
    doms, wavs, bits = lay.doms, lay.wavs, lay.bits
    blocks = atoms // BLOCK
    share = blocks // wavs
    inv_atoms = 1.0 / math.sqrt(atoms * doms)
    inv_waves = 1.0 / math.sqrt(KV)

    def swap(x, chain, step):
        pairs = []
        for d in range(doms):
            for w in range(wavs):
                pairs.append((d * wavs + w, (d ^ (1 << lay.order(w, chain)[step])) * wavs + w))
        return lax.ppermute(x, ("dom", "wav"), pairs)

    def swap_wav(x, mask):
        return lax.ppermute(x, "wav", [(w, w ^ mask) for w in range(wavs)])

    each = range(CHAINS)
    tables, positions, features = phase_tables(positions, features)
    phases_up, arrived = [], []
    for c in each:
        phases, leaving = spectrum_upper(lay, c, inv_atoms, tables, features)
        phases_up.append(phases)
        arrived.append(swap(leaving, c, 0))
    phases_low, kept = spectrum_lower(lay, inv_atoms, tables, features)

    if wavs == 2 and share == HALO_BLK:
        packed = pack_half(positions, features, share)
        count = doms * wavs
        chain = [(g, (g + 1 if g % 2 else g - 1) % count) for g in range(count)]
        halos = [lax.ppermute(packed, ("dom", "wav"), chain)]
    else:
        halos = side_halos(positions, features)
    short = short_range(neighbours, positions, features, halos, message_weight[0], share)

    sums = list(lattice_weights(lay, wavevectors, spectral_filter[0]))
    mask = wavs // 2
    while mask:
        others = [swap_wav(s, mask) for s in sums[mask:]]
        if mask == 1:
            sums = [sums[0], *others]
        else:
            sums = [add_plain(a, b) for a, b in zip(sums[:mask], others)]
        mask //= 2

    for step in range(1, bits - 1):
        for c in each:
            kept[c], leaving = add_split(kept[c], arrived[c])
            arrived[c] = swap(leaving, c, step)
    for c in each:
        kept[c], leaving = add_both(kept[c], arrived[c])
        arrived[c] = swap(leaving, c, bits - 1)
    filts = [filtered(c, kept[c], arrived[c], spectral_mix[0], sums) for c in each]
    for step in reversed(range(1, bits - 1)):
        for c in each:
            filts[c] = join(filts[c], swap(filts[c], c, step))
    filts_up = [swap(filts[c], c, 0) for c in each]
    part = back_lower(phases_low, filts)
    for c in range(CHAINS - 1):
        part = back_more(part, phases_up[c], filts_up[c])
    total, leaving = back_last(part, phases_up[-1], filts_up[-1], short, inv_waves)
    mask = wavs // 2
    while mask > 1:
        total = add_plain(total, swap_wav(total, mask))
        leaving = total
        mask //= 2
    return finish(features, total, swap_wav(leaving, 1))


def side_halos(positions, features):
    doms, atoms = lax.axis_size("dom"), features.shape[0]
    rim = HALO_BLK * BLOCK
    up = [(i, (i + 1) % doms) for i in range(doms)]
    down = [(j, i) for i, j in up]
    halos = []
    for at, pairs in ((atoms - rim, up), (0, down)):
        packed = pack_side(positions[:, at : at + rim], features[at : at + rim])
        halos.append(lax.ppermute(packed, "dom", pairs))
    return halos


def pack_side(positions, features):
    rows, channels = features.shape
    extra = -(-9 * HALO_BLK // (2 * TILE)) * 2 * TILE

    def body(pos_ref, h_ref, out_ref):
        out_ref[:rows, :] = h_ref[...]
        fill_coordinates(pos_ref[...], out_ref, rows)

    return call(body, VMEM((rows + extra, channels), BF16), positions, features)


def fill_coordinates(pos, out_ref, rows):
    high = pos.astype(BF16).astype(F32)
    mid = (pos - high).astype(BF16).astype(F32)
    parts = []
    for part in (high, mid, pos - high - mid):
        for axis in range(3):
            for b in range(rows // BLOCK):
                parts.append(part[axis : axis + 1, b * BLOCK : (b + 1) * BLOCK])
    parts += [jnp.zeros_like(parts[0])] * (out_ref.shape[0] - rows - len(parts))
    out_ref[rows:, :] = jnp.concatenate(parts, axis=0).astype(BF16)


def solution(mesh):
    placed = (
        P("dom", None),
        P(None, "dom"),
        P("dom", None),
        P(None, "wav"),
        P(),
        P(),
        P(None, "wav", None),
    )

    return jax.shard_map(local, mesh=mesh, in_specs=placed, out_specs=P("dom", None), check_vma=False)
```

```python
import math

import jax
import jax.numpy as jnp
from jax import lax
from jax.experimental import pallas as pl
from jax.experimental.pallas import tpu as pltpu
from jax.sharding import PartitionSpec as P


KV = 8192
BLOCK = 128
NBR = 8
HALO_BLK = 4
TOP = 8
SPAN = 2 * TOP + 1

TWO_PI = 2.0 * math.pi
KERNEL_DECAY = 12.0
DECAY_LOG2 = -KERNEL_DECAY * math.log2(math.e)
SPLIT = 64
PAIR_SCALE = 1.0 / 16.0

TILE = 8
CHAINS = 2
TURNS = (((2, 1, 0), (0, 1, 2)), ((0, 1, 2), (1, 2, 0)))
Q_TILES = 2 * SPAN + 3
Q_ROWS = Q_TILES * TILE
FIRST_TILE = 2 + 2 * TOP
ZERO_TILES = Q_TILES - FIRST_TILE
ALL_TILES = ZERO_TILES + TOP * Q_TILES
assert TOP == TILE

F32 = jnp.float32
BF16 = jnp.bfloat16
VMEM = pltpu.VMEM


def in_vmem(array):
    return pltpu.with_memory_space_constraint(array, VMEM)


def in_hbm(array):
    return pltpu.with_memory_space_constraint(array, pltpu.HBM)


def call(body, out, *args, smem=(), hbm=(), scratch=(), limit=16):
    spec = pl.BlockSpec(memory_space=VMEM)
    specs = [spec] * len(args) + [pl.BlockSpec(memory_space=pltpu.SMEM)] * len(smem)
    specs += [pl.BlockSpec(memory_space=pltpu.HBM)] * len(hbm)
    single = not isinstance(out, (list, tuple))
    return pl.pallas_call(
        body,
        in_specs=specs,
        out_specs=spec if single else [spec] * len(out),
        out_shape=out,
        scratch_shapes=list(scratch),
        compiler_params=pltpu.CompilerParams(vmem_limit_bytes=limit << 20),
    )(*[in_vmem(a) for a in args], *smem, *[in_hbm(a) for a in hbm])


DIVIDE = -(-(1 << 16) // Q_TILES)
assert all((v * DIVIDE) >> 16 == v // Q_TILES for v in range(FIRST_TILE + ALL_TILES))


class Layout:
    def __init__(self, atoms):
        self.atoms = atoms
        self.doms, self.wavs = lax.axis_size("dom"), lax.axis_size("wav")
        self.bits = self.doms.bit_length() - 1
        assert self.doms == 1 << self.bits and self.bits > 3
        assert self.wavs & (self.wavs - 1) == 0
        self.tiles = -(-ALL_TILES // (self.doms * self.wavs * CHAINS))
        self.slice_rows = 2 * TILE * self.tiles
        self.rows = self.slice_rows * self.doms

    def order(self, wav, chain):
        return [*TURNS[wav % 2][chain], *range(3, self.bits)]

    def code(self, wav, chain):
        dom = lax.axis_index("dom")
        codes = []
        for w in (0, 1):
            code = 0
            for step, bit in enumerate(self.order(w, chain)):
                code = code | (((dom >> bit) & 1) << (self.bits - 1 - step))
            codes.append(code)
        return jnp.where((wav & 1) == 0, codes[0], codes[1])

    def first_tile(self, wav, chain, position):
        number = CHAINS * wav + chain
        return (number * self.doms + (position ^ self.code(wav, chain))) * self.tiles


def tile_place(tile):
    tile = jnp.minimum(tile, ALL_TILES - 1) + FIRST_TILE
    n2 = (tile * DIVIDE) >> 16
    return n2, tile - n2 * Q_TILES


def times(a, b):
    return a[0] * b[0] - a[1] * b[1], a[0] * b[1] + a[1] * b[0]


def fill_tables(pos_ref, xyc_ref, xys_ref, zc_ref, zs_ref):
    angle = TWO_PI * pos_ref[...]
    power = [(jnp.ones_like(angle), jnp.zeros_like(angle)), (jnp.cos(angle), jnp.sin(angle))]
    for n in range(2, TOP + 1):
        power.append(times(power[n // 2], power[n - n // 2]))
    wide = (TILE, angle.shape[1])

    def row(n, axis):
        c, s = power[abs(n)]
        c, s = c[axis : axis + 1, :], s[axis : axis + 1, :]
        return c, (s if n >= 0 else -s)

    def spread(n, axis):
        return tuple(jnp.broadcast_to(v, wide) for v in row(n, axis))

    def stack(numbers, axis):
        rows = [row(n, axis) for n in numbers]
        return tuple(jnp.concatenate([r[i] for r in rows], axis=0) for i in (0, 1))

    for n in range(TOP + 1):
        at = slice(n * TILE, (n + 1) * TILE)
        zc_ref[at, :], zs_ref[at, :] = spread(n, 2)

    def put(tile, a, b):
        at = slice(tile * TILE, (tile + 1) * TILE)
        xyc_ref[at, :], xys_ref[at, :] = times(a, b)

    below, above = stack(range(-TOP, 0), 1), stack(range(TOP), 1)
    edge = spread(TOP, 1)
    for n in range(-TOP, TOP + 1):
        here = spread(n, 0)
        put(1 + 2 * (n + TOP), here, below)
        put(2 + 2 * (n + TOP), here, above)
    put(0, stack(range(-TOP, 0), 0), edge)
    put(Q_TILES - 2, stack(range(TOP), 0), edge)
    put(Q_TILES - 1, spread(TOP, 0), edge)


def fill_phases(lay, chain, low, count, tables, h_ref, p_ref, p_at, put):
    xyc_ref, xys_ref, zc_ref, zs_ref = tables
    wav = lax.axis_index("wav")
    group = max(1, count // 2)
    rows = group * lay.slice_rows
    feats = h_ref[...]

    for step in range(count // group):
        start = p_at + step * rows
        for part in range(group):
            base = lay.first_tile(wav, chain, low + step * group + part)
            for i in range(lay.tiles):
                n2, qt = tile_place(base + i)
                q_at = pl.ds(pl.multiple_of(qt * TILE, TILE), TILE)
                z_at = pl.ds(pl.multiple_of(n2 * TILE, TILE), TILE)
                c, s = times((xyc_ref[q_at, :], xys_ref[q_at, :]), (zc_ref[z_at, :], zs_ref[z_at, :]))
                at = start + (part * lay.tiles + i) * 2 * TILE
                p_ref[at : at + 2 * TILE, :] = jnp.concatenate([c, s], axis=0).astype(BF16)
        here = slice(start, start + rows)
        at = slice(step * rows, (step + 1) * rows)
        put(at, jnp.dot(p_ref[here, :], feats, preferred_element_type=F32))


def phase_tables(positions, features):
    atoms = positions.shape[1]
    table = [(Q_ROWS, atoms)] * 2 + [((TOP + 1) * TILE, atoms)] * 2

    def body(pos_hbm, h_hbm, *refs):
        *table_refs, pos_ref, h_ref, sems = refs
        bring_pos = pltpu.make_async_copy(pos_hbm, pos_ref, sems.at[0])
        bring_h = pltpu.make_async_copy(h_hbm, h_ref, sems.at[1])
        bring_pos.start()
        bring_h.start()
        bring_pos.wait()
        fill_tables(pos_ref, *table_refs)
        bring_h.wait()

    out = [VMEM(shape, F32) for shape in table]
    out += [VMEM(positions.shape, F32), VMEM(features.shape, BF16)]
    *tables, pos, h = call(
        body, out, hbm=[positions, features],
        scratch=[pltpu.SemaphoreType.DMA((2,))],
    )
    return tables, pos, h


def spectrum_upper(lay, chain, scale, tables, features):
    half = lay.doms // 2

    def body(xyc, xys, zc, zs, h_ref, p_ref, s_ref):
        def put(at, value):
            s_ref[at, :] = (value * scale).astype(BF16)

        fill_phases(lay, chain, half, half, (xyc, xys, zc, zs), h_ref, p_ref, 0, put)

    out = [VMEM((lay.rows // 2, lay.atoms), BF16), VMEM((lay.rows // 2, features.shape[1]), BF16)]
    return call(body, out, *tables, features)


def spectrum_lower(lay, scale, tables, features):
    def body(xyc, xys, zc, zs, h_ref, p_ref, *s_refs):
        for chain, s_ref in enumerate(s_refs):

            def put(at, value):
                s_ref[at, :] = value * scale

            fill_phases(
                lay, chain, 0, lay.doms // 2, (xyc, xys, zc, zs), h_ref, p_ref,
                chain * (lay.rows // 2), put,
            )

    out = [VMEM((CHAINS * lay.rows // 2, lay.atoms), BF16)]
    out += [VMEM((lay.rows // 2, features.shape[1]), F32)] * CHAINS
    phases, *sums = call(body, out, *tables, features)
    return phases, sums


def lattice_weights(lay, wavevectors, weights):
    waves, channels = weights.shape
    tiles = 2 * lay.tiles * lay.wavs * CHAINS
    chunk = min(waves, 1024)

    def body(wave_ref, filter_ref, *refs):
        *out_refs, hot_ref = refs
        wav = lax.axis_index("wav")
        bases = []
        for v in range(lay.wavs):
            for chain in range(CHAINS):
                for p in range(2):
                    first = lay.first_tile(wav ^ v, chain, p)
                    for i in range(lay.tiles):
                        n2, qt = tile_place(first + i)
                        base = n2 * Q_ROWS + qt * TILE
                        bases.append(jnp.where(first + i < ALL_TILES, base, -Q_ROWS))
        total = None
        for start in range(0, waves, chunk):
            at = slice(start, start + chunk)
            n0, n1, n2 = (wave_ref[a : a + 1, at] for a in range(3))
            negative = jnp.logical_or(n0 < 0, jnp.logical_and(n0 == 0, n1 < 0))
            flip = jnp.logical_or(n2 < 0, jnp.logical_and(n2 == 0, negative))
            n0, n1, n2 = (jnp.where(flip, -n, n) for n in (n0, n1, n2))
            inner = TILE + (n0 + TOP) * 2 * TILE + n1 + TOP
            outer = jnp.where(n0 < 0, n0 + TOP, (Q_TILES - 2) * TILE + n0)
            key = n2 * Q_ROWS + jnp.where(n1 == TOP, outer, inner)
            wide = jnp.broadcast_to(key, (TILE, chunk))
            shifted = wide - lax.broadcasted_iota(jnp.int32, wide.shape, 0)
            for t in range(0, tiles, 2):
                both = [jnp.where(shifted == bases[u], 1.0, 0.0) for u in (t, t + 1)]
                hot_ref[t * TILE : (t + 2) * TILE, :] = jnp.concatenate(both, axis=0).astype(BF16)
            w = filter_ref[at, :]
            high = w.astype(BF16)
            low = (w - high.astype(F32)).astype(BF16)
            part = jnp.dot(
                hot_ref[...], jnp.concatenate([high, low], axis=1), preferred_element_type=F32
            )
            total = part if total is None else total + part
        total = total[:, :channels] + total[:, channels:]
        rows = tiles * TILE // lay.wavs
        for v, ref in enumerate(out_refs):
            ref[...] = total[v * rows : (v + 1) * rows]

    out = [VMEM((tiles * TILE // lay.wavs, channels), F32)] * lay.wavs
    return call(
        body, out, wavevectors, weights,
        scratch=[VMEM((tiles * TILE, chunk), BF16)],
    )


def add_split(mine, other):
    rows, channels = mine.shape

    def body(a_ref, b_ref, keep_ref, send_ref):
        total = a_ref[...] + b_ref[...].astype(F32)
        keep_ref[...] = total[: rows // 2]
        send_ref[...] = total[rows // 2 :].astype(BF16)

    out = [VMEM((rows // 2, channels), F32), VMEM((rows // 2, channels), BF16)]
    return call(body, out, mine, other)


def add_both(mine, other):
    def body(a_ref, b_ref, keep_ref, send_ref):
        total = a_ref[...] + b_ref[...].astype(F32)
        keep_ref[...] = total
        send_ref[...] = total.astype(BF16)

    return call(body, [VMEM(mine.shape, t) for t in (F32, BF16)], mine, other)


def add_plain(mine, other):
    def body(a_ref, b_ref, out_ref):
        out_ref[...] = a_ref[...] + b_ref[...].astype(F32)

    return call(body, VMEM(mine.shape, F32), mine, other)


def dot_exact(a, b):
    return jnp.dot(a, b, precision=lax.Precision.HIGHEST, preferred_element_type=F32)


def filtered(chain, mine, other, mixing, weights):
    rows, channels = mine.shape
    half = rows // 2
    groups = rows // (2 * TILE)

    def body(mine_ref, other_ref, mix_ref, *refs):
        *weight_refs, out_ref = refs
        there = other_ref[...].astype(F32)
        total = mine_ref[...] + jnp.concatenate([there[half:], there[:half]], axis=0)
        mixed = dot_exact(total, mix_ref[...])
        at = slice(chain * half, (chain + 1) * half)
        factor = weight_refs[0][at, :]
        for ref in weight_refs[1:]:
            factor = factor + ref[at, :]
        mixed = mixed.reshape(groups, 2, TILE, channels) * factor.reshape(groups, 1, TILE, channels)
        out_ref[...] = mixed.reshape(rows, channels).astype(BF16)

    return call(body, VMEM(mine.shape, BF16), mine, other, mixing, *weights)


def join(low, high):
    def body(a_ref, b_ref, out_ref):
        rows = a_ref.shape[0]
        out_ref[:rows, :] = a_ref[...]
        out_ref[rows:, :] = b_ref[...]

    out = VMEM((low.shape[0] + high.shape[0], low.shape[1]), low.dtype)
    return call(body, out, low, high)


def pack_half(positions, features, share):
    rows, channels = share * BLOCK, features.shape[1]
    extra = -(-9 * share // (2 * TILE)) * 2 * TILE

    def body(pos_ref, h_ref, out_ref):
        start = pl.multiple_of(lax.axis_index("wav") * rows, rows)
        out_ref[:rows, :] = h_ref[pl.ds(start, rows), :]
        fill_coordinates(pos_ref[:, pl.ds(start, rows)], out_ref, rows)

    return call(body, VMEM((rows + extra, channels), BF16), positions, features)


def short_range(neighbours, positions, features, halos, weight, share):
    channels = features.shape[1]
    own = features.shape[0] // BLOCK
    near = [HALO_BLK] * len(halos)
    blocks = own + sum(near)
    both = len(halos) == 2

    def body(pos_ref, h_ref, weight_ref, *refs):
        halo_refs, (lists, out_ref, val_ref, at_ref) = refs[: len(halos)], refs[len(halos) :]
        w = weight_ref[...]

        def project(rows):
            return jnp.dot(rows, w, preferred_element_type=F32).astype(BF16)

        val_ref[: own * BLOCK, :] = project(h_ref[...])
        pos = pos_ref[...]
        for b in range(own):
            at_ref[b, 0:3, :] = pos[:, b * BLOCK : (b + 1) * BLOCK]
        at = own
        for ref, count in zip(halo_refs, near):
            rows = count * BLOCK
            val_ref[at * BLOCK : (at + count) * BLOCK, :] = project(ref[:rows, :])
            pieces = ref[rows:, :].astype(F32)
            n = 3 * count
            there = pieces[:n] + pieces[n : 2 * n] + pieces[2 * n : 3 * n]
            for b in range(count):
                for axis in range(3):
                    k = axis * count + b
                    at_ref[at + b, axis : axis + 1, :] = there[k : k + 1]
            at += count
        first = lax.axis_index("wav") * share

        def block(b, carry):
            columns = jnp.transpose(at_ref[first + b])
            total = jnp.zeros((BLOCK, channels), F32)
            for m in range(NBR):
                ext = lists[first + b, m]
                inside = jnp.logical_and(ext >= HALO_BLK, ext < HALO_BLK + own)
                if both:
                    outside = own + jnp.where(ext < HALO_BLK, ext, ext - own)
                else:
                    outside = own + jnp.where(ext < HALO_BLK, ext, ext - HALO_BLK - own)
                sender = jnp.where(inside, ext - HALO_BLK, outside)
                sent = at_ref[sender]
                parts = []
                for low in range(0, BLOCK, SPLIT):
                    distance = None
                    for axis in range(3):
                        here = columns[low : low + SPLIT, axis : axis + 1]
                        delta = here - sent[axis : axis + 1, :]
                        delta = delta - jnp.round(delta)
                        square = delta * delta
                        distance = square if distance is None else distance + square
                    parts.append(jnp.exp2(distance * DECAY_LOG2).astype(BF16))
                kernel = jnp.concatenate(parts, axis=0)
                rows = pl.ds(pl.multiple_of(sender * BLOCK, BLOCK), BLOCK)
                total = total + jnp.dot(kernel, val_ref[rows, :], preferred_element_type=F32)
            out_ref[pl.ds(pl.multiple_of(b * BLOCK, BLOCK), BLOCK), :] = total * PAIR_SCALE
            return carry

        lax.fori_loop(0, share, block, 0, unroll=True)

    return call(
        body, VMEM((share * BLOCK, channels), F32), positions, features, weight,
        *halos, smem=[neighbours],
        scratch=[VMEM((blocks * BLOCK, channels), BF16), VMEM((blocks, TILE, BLOCK), F32)],
    )


def transposed_dot(phases, filt):
    dims = (((0,), (0,)), ((), ()))
    return lax.dot_general(phases, filt, dims, preferred_element_type=F32)


def back_lower(phases, filts):
    def body(p_ref, *refs):
        *f_refs, out_ref = refs
        filt = jnp.concatenate([ref[...] for ref in f_refs], axis=0)
        out_ref[...] = transposed_dot(p_ref[...], filt)

    out = VMEM((phases.shape[1], filts[0].shape[1]), F32)
    return call(body, out, phases, *filts)


def back_more(part, phases, filt):
    def body(part_ref, p_ref, f_ref, out_ref):
        out_ref[...] = part_ref[...] + transposed_dot(p_ref[...], f_ref[...])

    return call(body, VMEM(part.shape, F32), part, phases, filt)


def back_last(part, phases, filt, short, scale):
    rows = short.shape[0]

    def body(part_ref, p_ref, f_ref, short_ref, out_ref, send_ref):
        out_ref[...] = (part_ref[...] + transposed_dot(p_ref[...], f_ref[...])) * scale
        here = pl.ds(pl.multiple_of(lax.axis_index("wav") * rows, rows), rows)
        out_ref[here, :] += short_ref[...]
        send_ref[...] = out_ref[...].astype(BF16)

    out = [VMEM(part.shape, t) for t in (F32, BF16)]
    return call(body, out, part, phases, filt, short)


def finish(features, total, other):
    def body(h_ref, a_ref, b_ref, out_ref):
        total = a_ref[...] + b_ref[...].astype(F32)
        out_ref[...] = (h_ref[...].astype(F32) + total * jax.nn.sigmoid(total)).astype(BF16)

    out = jax.ShapeDtypeStruct(features.shape, BF16)
    return call(body, out, features, total, other)


def local(
    node_features, positions, neighbours, wavevectors, message_weight, spectral_mix, spectral_filter
):
    features = node_features
    atoms = features.shape[0]
    lay = Layout(atoms)
    doms, wavs, bits = lay.doms, lay.wavs, lay.bits
    blocks = atoms // BLOCK
    share = blocks // wavs
    inv_atoms = 1.0 / math.sqrt(atoms * doms)
    inv_waves = 1.0 / math.sqrt(KV)

    def swap(x, chain, step):
        pairs = []
        for d in range(doms):
            for w in range(wavs):
                pairs.append((d * wavs + w, (d ^ (1 << lay.order(w, chain)[step])) * wavs + w))
        return lax.ppermute(x, ("dom", "wav"), pairs)

    def swap_wav(x, mask):
        return lax.ppermute(x, "wav", [(w, w ^ mask) for w in range(wavs)])

    each = range(CHAINS)
    tables, positions, features = phase_tables(positions, features)
    phases_up, arrived = [], []
    for c in each:
        phases, leaving = spectrum_upper(lay, c, inv_atoms, tables, features)
        phases_up.append(phases)
        arrived.append(swap(leaving, c, 0))
    phases_low, kept = spectrum_lower(lay, inv_atoms, tables, features)

    if wavs == 2 and share == HALO_BLK:
        packed = pack_half(positions, features, share)
        count = doms * wavs
        chain = [(g, (g + 1 if g % 2 else g - 1) % count) for g in range(count)]
        halos = [lax.ppermute(packed, ("dom", "wav"), chain)]
    else:
        halos = side_halos(positions, features)
    short = short_range(neighbours, positions, features, halos, message_weight[0], share)

    sums = list(lattice_weights(lay, wavevectors, spectral_filter[0]))
    mask = wavs // 2
    while mask:
        others = [swap_wav(s, mask) for s in sums[mask:]]
        if mask == 1:
            sums = [sums[0], *others]
        else:
            sums = [add_plain(a, b) for a, b in zip(sums[:mask], others)]
        mask //= 2

    for step in range(1, bits - 1):
        for c in each:
            kept[c], leaving = add_split(kept[c], arrived[c])
            arrived[c] = swap(leaving, c, step)
    for c in each:
        kept[c], leaving = add_both(kept[c], arrived[c])
        arrived[c] = swap(leaving, c, bits - 1)
    filts = [filtered(c, kept[c], arrived[c], spectral_mix[0], sums) for c in each]
    for step in reversed(range(1, bits - 1)):
        for c in each:
            filts[c] = join(filts[c], swap(filts[c], c, step))
    filts_up = [swap(filts[c], c, 0) for c in each]
    part = back_lower(phases_low, filts)
    for c in range(CHAINS - 1):
        part = back_more(part, phases_up[c], filts_up[c])
    total, leaving = back_last(part, phases_up[-1], filts_up[-1], short, inv_waves)
    mask = wavs // 2
    while mask > 1:
        total = add_plain(total, swap_wav(total, mask))
        leaving = total
        mask //= 2
    return finish(features, total, swap_wav(leaving, 1))


def side_halos(positions, features):
    doms, atoms = lax.axis_size("dom"), features.shape[0]
    rim = HALO_BLK * BLOCK
    up = [(i, (i + 1) % doms) for i in range(doms)]
    down = [(j, i) for i, j in up]
    halos = []
    for at, pairs in ((atoms - rim, up), (0, down)):
        packed = pack_side(positions[:, at : at + rim], features[at : at + rim])
        halos.append(lax.ppermute(packed, "dom", pairs))
    return halos


def pack_side(positions, features):
    rows, channels = features.shape
    extra = -(-9 * HALO_BLK // (2 * TILE)) * 2 * TILE

    def body(pos_ref, h_ref, out_ref):
        out_ref[:rows, :] = h_ref[...]
        fill_coordinates(pos_ref[...], out_ref, rows)

    return call(body, VMEM((rows + extra, channels), BF16), positions, features)


def fill_coordinates(pos, out_ref, rows):
    high = pos.astype(BF16).astype(F32)
    mid = (pos - high).astype(BF16).astype(F32)
    parts = []
    for part in (high, mid, pos - high - mid):
        for axis in range(3):
            for b in range(rows // BLOCK):
                parts.append(part[axis : axis + 1, b * BLOCK : (b + 1) * BLOCK])
    parts += [jnp.zeros_like(parts[0])] * (out_ref.shape[0] - rows - len(parts))
    out_ref[rows:, :] = jnp.concatenate(parts, axis=0).astype(BF16)


def solution(mesh):
    placed = (
        P("dom", None),
        P(None, "dom"),
        P("dom", None),
        P(None, "wav"),
        P(),
        P(),
        P(None, "wav", None),
    )

    return jax.shard_map(local, mesh=mesh, in_specs=placed, out_specs=P("dom", None), check_vma=False)
```
